32 devices in a mesh: gx: 8 (over z, x), gy: 4 (over y, core).
Axes of the slice: x: 2, y: 2, z: 4, core: 2. Of those that a mesh axis runs over, the one named last changes fastest.
Arguments:
- phase_frac: float32 [8, 64, 64, 128], P(None, 'gx', 'gy'), may hold values from 0 to 1, as said below
- phase_ids: int32 [8, 64, 64, 128], P(None, 'gx', 'gy'), may hold values from 0 to 15, as said below
- conc: float32 [64, 64, 128], P('gx', 'gy'), may hold values from -6 to 6
- pair_class: int32 [16, 16], replicated, may hold values from 0 to 3, as said below
- mobility: float32 [4], replicated, may hold values from 0.01 to 0.06
- drive: float32 [16], replicated, may hold values from -4 to 4
- diffusivity: float32 [16], replicated, may hold values from 8 to 800
Outputs:
- new_frac: float32 [8, 64, 64, 128], P(None, 'gx', 'gy')
- new_conc: float32 [64, 64, 128], P('gx', 'gy')
The draws below stay inside these ranges and needn't reach their ends.
Inputs may be any that keep to these rules, and one draw needn't show every extreme that they name: `phase_frac`: for every voxel the 8 fractions are positive and sum to 1. `phase_ids`: the 8 ids of one voxel are distinct. `pair_class`: Symmetric.
All inputs are finite; a program needn't handle non-finite values.
Results may differ from the reference program's by a relative error of at most 0.0003.
Values sent between devices are 32-bit elements; how exact they have to be, the bound alone decides.
No kernel may reach another device: no remote copies, remote signals or barrier semaphores. Data moves between devices by JAX's collectives and lax.ppermute only.
A program may use at most 64 MiB of HBM per device.

```python
import math
import jax
import jax.numpy as jnp
from jax import lax

SLOTS = 8
NPH = 16
NCLS = 4
NX = 64
NY = 64
NZ = 128


def draw_phase_frac(key, part):
    inner = jax.random.fold_in(key, 7)
    weights = jax.random.uniform(inner, (SLOTS, NX, NY, NZ), jnp.float32, 0.05, 1.0)
    return (weights / jnp.sum(weights, axis=0, keepdims=True)).astype(jnp.float32)


def draw_phase_ids(key, part):
    first, second, third = jax.random.split(jax.random.fold_in(key, 11), 3)
    xs = jnp.arange(NX, dtype=jnp.int32)[:, None, None]
    ys = jnp.arange(NY, dtype=jnp.int32)[None, :, None]
    zs = jnp.arange(NZ, dtype=jnp.int32)[None, None, :]
    region = xs // 5 + ys // 7 + zs // 11
    jitter = jax.random.randint(first, (NX, NY, NZ), 0, 3)
    turning = jax.random.randint(second, (NX, NY, NZ), 0, SLOTS)
    order = jax.random.permutation(third, NPH)
    slot_list = jnp.arange(SLOTS, dtype=jnp.int32)[:, None, None, None]
    base = (region + jitter)[None] + (slot_list + turning[None]) % SLOTS
    return order[base % NPH].astype(jnp.int32)


def draw_pair_class(key, part):
    table = jax.random.randint(jax.random.fold_in(key, 13), (NPH, NPH), 0, NCLS)
    return ((table + table.T) % NCLS).astype(jnp.int32)


def shard_levels(stream_key, dims, cuts, least, top_value):
    factor_of = 1.0
    for position, shards_of in cuts:
        steps = jax.random.uniform(jax.random.fold_in(jax.random.fold_in(stream_key, 6), position), (shards_of,), jnp.float32, least / len(cuts), top_value / len(cuts))
        factor_of = factor_of * jnp.repeat(jnp.exp(steps), dims[position] // shards_of).reshape((-1,) + (1,) * (len(dims) - 1 - position))
    return factor_of


def scatter_about(stream_key, dims, scale, limit, cuts=(), kind=jnp.bfloat16):
    loudness = shard_levels(stream_key, dims, cuts, -0.22, 0.18) if cuts else 1.0
    array = jax.random.normal(stream_key, dims, jnp.float32) * scale * loudness
    return jnp.minimum(jnp.maximum(array, -limit), limit).astype(kind)


def setup_inputs(seed: int = 0) -> dict:
    seeds = jax.random.split(jax.random.key(seed), 8)
    phase_frac = draw_phase_frac(jax.random.fold_in(seeds[7], 71), 0)
    phase_ids = draw_phase_ids(jax.random.fold_in(seeds[7], 71), 0)
    conc = scatter_about(seeds[2], (NX, NY, NZ), 1.0, 6.0, ((0, 8), (1, 4)), jnp.float32)
    pair_class = draw_pair_class(jax.random.fold_in(seeds[7], 71), 0)
    mobility = jnp.clip(jnp.exp(jax.random.uniform(seeds[4], (NCLS,), jnp.float32, math.log(0.01), math.log(0.06))), 0.01, 0.06)
    drive = scatter_about(seeds[5], (NPH,), 1.0, 4.0, (), jnp.float32)
    diffusivity = jnp.clip(jnp.exp(jax.random.uniform(seeds[6], (NPH,), jnp.float32, math.log(8.0), math.log(800.0))), 8.0, 800.0)
    return dict(phase_frac=phase_frac, phase_ids=phase_ids, conc=conc, pair_class=pair_class, mobility=mobility, drive=drive, diffusivity=diffusivity)


KAPPA = 2.0
DRIVE = 4.0


def thomas(sub_diag, main_diag, super_diag, rhs_lines):
    sub_diag = jnp.broadcast_to(sub_diag, rhs_lines.shape)
    main_diag = jnp.broadcast_to(main_diag, rhs_lines.shape)
    super_diag = jnp.broadcast_to(super_diag, rhs_lines.shape)
    anchor = jnp.zeros(rhs_lines.shape[1:], jnp.float32)

    def forward(running, coeffs):
        ratio_prev, value_prev = running
        sub_term, main_term, super_term, source_term = coeffs
        pivot_term = main_term - sub_term * ratio_prev
        ratio_now = super_term / pivot_term
        value_now = (source_term - sub_term * value_prev) / pivot_term
        return (ratio_now, value_now), (ratio_now, value_now)

    _, (ratios, values) = lax.scan(forward, (anchor, anchor), (sub_diag, main_diag, super_diag, rhs_lines))

    def backward(following, coeffs):
        ratio_now, value_now = coeffs
        current = value_now - ratio_now * following
        return current, current

    _, solved = lax.scan(backward, anchor, (ratios, values), reverse=True)
    return solved


def line_parts(diffus, field):
    face = 0.5 * (diffus[1:] + diffus[:-1])
    flux = face * (field[1:] - field[:-1])
    border = jnp.zeros_like(face[:1])
    face_left = jnp.concatenate([border, face])
    face_right = jnp.concatenate([face, border])
    flux_left = jnp.concatenate([border, flux])
    flux_right = jnp.concatenate([flux, border])
    return flux_right - flux_left, -face_left, 1.0 + face_left + face_right, -face_right


def along(diffus, field, axis_number):
    applied, sub_diag, main_diag, super_diag = line_parts(jnp.moveaxis(diffus, axis_number, 0), jnp.moveaxis(field, axis_number, 0))
    return jnp.moveaxis(applied, 0, axis_number), (sub_diag, main_diag, super_diag)


def solve_along(coeffs, source, axis_number):
    solved = thomas(coeffs[0], coeffs[1], coeffs[2], jnp.moveaxis(source, axis_number, 0))
    return jnp.moveaxis(solved, 0, axis_number)


def reference(phase_frac, phase_ids, conc, pair_class, mobility, drive, diffusivity):
    classes = jnp.arange(NCLS, dtype=jnp.int32)
    mob_table = jnp.sum(jnp.where(pair_class[:, :, None] == classes, mobility, 0.0), axis=2)
    dense = jnp.stack([jnp.sum(jnp.where(phase_ids == phase, phase_frac, 0.0), axis=0) for phase in range(NPH)])
    neighbours = ((jnp.roll(dense, -1, 1) + jnp.roll(dense, 1, 1)) + (jnp.roll(dense, -1, 2) + jnp.roll(dense, 1, 2))) + (jnp.roll(dense, -1, 3) + jnp.roll(dense, 1, 3))
    lap_dense = neighbours - 6.0 * dense
    curvature = jnp.take_along_axis(lap_dense, phase_ids, axis=0)
    drive_slot = drive[phase_ids]
    diff_slot = diffusivity[phase_ids]
    level = curvature + KAPPA * phase_frac
    pieces = []
    for slot_index in range(SLOTS):
        pair_mob = mob_table[phase_ids[slot_index][None], phase_ids]
        term = (level[slot_index] - level) + DRIVE * phase_frac[slot_index] * phase_frac * (drive_slot[slot_index] - drive_slot) * conc
        pieces.append(jnp.sum(pair_mob * term, axis=0))
    new_frac = phase_frac + jnp.stack(pieces)
    diffus = 1.0 + jnp.sum(new_frac * new_frac * diff_slot, axis=0)
    apply_x, coeffs_x = along(diffus, conc, 0)
    apply_y, coeffs_y = along(diffus, conc, 1)
    apply_z, coeffs_z = along(diffus, conc, 2)
    section_x = solve_along(coeffs_x, conc + apply_y + apply_z, 0)
    section_y = solve_along(coeffs_y, section_x - apply_y, 1)
    new_conc = solve_along(coeffs_z, section_y - apply_z, 2)
    return new_frac, new_conc
```

```python
import functools

import jax
import jax.numpy as jnp
from jax import lax
from jax.experimental import pallas as pl
from jax.experimental.pallas import tpu as pltpu
from jax.sharding import PartitionSpec as P

KAPPA = 2.0
DRIVE = 4.0
SUB = 8

VMEM = pl.BlockSpec(memory_space=pltpu.VMEM)
SMEM = pl.BlockSpec(memory_space=pltpu.SMEM)


def call(kernel, name, outs, ins, scratch=(), aliases={}, cost=20000, scalars=()):
    f32 = jnp.float32
    return pl.pallas_call(
        kernel,
        name=name,
        out_shape=[jax.ShapeDtypeStruct(s, f32) for s in outs],
        in_specs=[SMEM if i in scalars else VMEM for i in range(len(ins))],
        out_specs=[VMEM] * len(outs),
        scratch_shapes=[pltpu.VMEM(s, f32) for s in scratch],
        input_output_aliases=aliases,
        compiler_params=pltpu.CompilerParams(vmem_limit_bytes=12 << 20),
        cost_estimate=pl.CostEstimate(flops=cost * 1000, bytes_accessed=1 << 20, transcendentals=0),
    )(*ins)


def lookup(table, index):
    dims = lax.GatherDimensionNumbers(
        offset_dims=(),
        collapsed_slice_dims=(1,),
        start_index_map=(1,),
        operand_batching_dims=(0,),
        start_indices_batching_dims=(0,),
    )
    return lax.gather(
        table, index[..., None], dims, (1, 1), mode=lax.GatherScatterMode.PROMISE_IN_BOUNDS
    )


def scalar_table(ref, shape):
    lane = lax.broadcasted_iota(jnp.int32, shape, 1)
    table = jnp.zeros(shape, jnp.float32)
    for k in range(ref.shape[0]):
        table = jnp.where(lane == k, ref[k], table)
    return table


def even(axis):
    return lax.rem(lax.axis_index(axis), 2) == 0


def pick_rows(ids, fields, count):
    rows = []
    for phase in range(count):
        total = jnp.zeros(fields[0].shape, jnp.float32)
        for slot_id, field in zip(ids, fields):
            total = jnp.where(slot_id == phase, field, total)
        rows.append(total)
    return rows


def pick_slots(ids, rows):
    picked = [jnp.zeros(ids[0].shape, jnp.float32) for _ in ids]
    for phase, row in enumerate(rows):
        picked = [jnp.where(i == phase, row, t) for i, t in zip(ids, picked)]
    return picked


def exchange(level, ids, tables, phases, source=None):
    width = tables.shape[1]
    per_row = width // phases
    count = tables.shape[0] // SUB
    lane_of = [lax.rem(i, per_row) * phases if per_row & (per_row - 1) else (i & (per_row - 1)) * phases for i in ids]
    sums = [jnp.zeros(level[0].shape, jnp.float32) for _ in level]
    for a in range(len(level)):
        above = [ids[a] >= t * per_row for t in range(1, count)]
        for b in range(a + 1, len(level)):
            index = lane_of[a] + ids[b]
            mob = lookup(tables[0:SUB], index)
            for t in range(1, count):
                mob = jnp.where(above[t - 1], lookup(tables[t * SUB : (t + 1) * SUB], index), mob)
            term = level[a] - level[b]
            if source is not None:
                frac, drive, conc = source
                term = term + (conc * frac[a]) * (frac[b] * (drive[a] - drive[b]))
            term = mob * term
            sums[a] = sums[a] + term
            sums[b] = sums[b] - term
    return sums


def faces_kernel(phases, shape, frac, ids, conc, x_a, x_b, y_a, y_b):
    nx, ny, _ = shape
    slots = frac.shape[0]
    right = even("gx")
    for out, upper in ((x_a, right), (x_b, jnp.logical_not(right))):
        base = jnp.where(upper, (nx - 1) * ny, 0)
        for part in range(ny // SUB):
            rows = pl.ds(pl.multiple_of(base + part * SUB, SUB), SUB)
            held = pick_rows(
                [ids[s, rows, :] for s in range(slots)],
                [frac[s, rows, :] for s in range(slots)],
                phases,
            )
            for phase in range(phases):
                out[phase, part * SUB : (part + 1) * SUB, :] = held[phase]
    up = even("gy")
    for out, upper in ((y_a, up), (y_b, jnp.logical_not(up))):
        rows = pl.ds(jnp.where(upper, ny - 1, 0), nx, stride=ny)
        held = pick_rows(
            [ids[s, rows, :] for s in range(slots)],
            [frac[s, rows, :] for s in range(slots)],
            phases,
        )
        for phase in range(phases):
            out[phase] = held[phase]
        out[phases] = conc[rows, :]


def interior_kernel(
    phases, shape, frac, ids, conc, pair_class, mobility, drive, diffusivity,
    new_out, diff_out, table_out, dense,
):
    nx, ny, nz = shape
    slots = frac.shape[0]
    pitch = ny + 2 * SUB
    parts = ny // SUB
    per_row = nz // phases
    count = -(-phases // per_row)
    lane = lax.broadcasted_iota(jnp.int32, (per_row, nz), 1)
    row = lax.broadcasted_iota(jnp.int32, (per_row, nz), 0)
    for t in range(count):
        block = pair_class[t * per_row : (t + 1) * per_row, :]
        wide = jnp.concatenate([block] * per_row, axis=1)
        values = jnp.zeros(wide.shape, jnp.float32)
        for k in range(mobility.shape[0]):
            values = jnp.where(wide == k, mobility[k], values)
        line = jnp.sum(
            jnp.where((lane >= row * phases) & (lane < (row + 1) * phases), values, 0.0),
            axis=0,
            keepdims=True,
        )
        table_out[t * SUB : (t + 1) * SUB, :] = jnp.broadcast_to(line, (SUB, nz))
    drive_table = scalar_table(drive, (SUB, nz))
    diff_table = scalar_table(diffusivity, (SUB, nz))
    nothing = jnp.zeros((SUB, nz), jnp.float32)

    def clear(phase, carry):
        for plane in range(nx + 2):
            for part in range(parts + 2):
                if plane in (0, nx + 1) or part in (0, parts + 1):
                    dense[phase, plane * pitch + part * SUB : plane * pitch + (part + 1) * SUB, :] = nothing
        return carry

    lax.fori_loop(0, phases, clear, 0)

    def build(x, carry):
        for part in range(parts):
            rows = pl.ds(pl.multiple_of(x * ny, SUB) + part * SUB, SUB)
            held = pick_rows(
                [ids[s, rows, :] for s in range(slots)],
                [frac[s, rows, :] for s in range(slots)],
                phases,
            )
            into = pl.ds(pl.multiple_of((x + 1) * pitch, SUB) + (part + 1) * SUB, SUB)
            for phase in range(phases):
                dense[phase, into, :] = held[phase]
        return carry

    lax.fori_loop(0, nx, build, 0)

    def update(x, carry):
        for part in range(parts):
            rows = pl.ds(pl.multiple_of(x * ny, SUB) + part * SUB, SUB)
            at = pl.multiple_of((x + 1) * pitch, SUB) + (part + 1) * SUB

            def laplacian():
                for phase in range(phases):
                    centre = dense[phase, pl.ds(at, SUB), :]
                    along_x = dense[phase, pl.ds(at + pitch, SUB), :] + dense[phase, pl.ds(at - pitch, SUB), :]
                    along_y = dense[phase, pl.ds(at + 1, SUB), :] + dense[phase, pl.ds(at - 1, SUB), :]
                    along_z = pltpu.roll(centre, nz - 1, 1) + pltpu.roll(centre, 1, 1)
                    yield (along_x + along_y + along_z) - 6.0 * centre

            slot_ids = [ids[s, rows, :] for s in range(slots)]
            curvature = pick_slots(slot_ids, laplacian())
            slot_frac = [frac[s, rows, :] for s in range(slots)]
            level = [c + KAPPA * f for c, f in zip(curvature, slot_frac)]
            slot_drive = [lookup(drive_table, i) for i in slot_ids]
            sums = exchange(
                level, slot_ids, table_out, phases, (slot_frac, slot_drive, DRIVE * conc[rows, :])
            )
            diffus = jnp.ones((SUB, nz), jnp.float32)
            for s in range(slots):
                new = slot_frac[s] + sums[s]
                new_out[s, rows, :] = new
                diffus = diffus + new * new * lookup(diff_table, slot_ids[s])
            diff_out[rows, :] = diffus
        return carry

    lax.fori_loop(0, nx, update, 0)


def outer_kernel(
    phases, shape, new_in, diff_in, table, ids, x_a, x_b, y_a, y_b, diffusivity,
    new_out, diff_out, face_a, face_b,
):
    nx, ny, nz = shape
    slots = new_in.shape[0]
    diff_table = scalar_table(diffusivity, (SUB, nz))
    new_out[...] = new_in[...]
    diff_out[...] = diff_in[...]

    def add(rows, halo):
        slot_ids = [ids[s, rows, :] for s in range(slots)]
        level = pick_slots(slot_ids, (halo(p) for p in range(phases)))
        sums = exchange(level, slot_ids, table, phases)
        diffus = jnp.ones(sums[0].shape, jnp.float32)
        for s in range(slots):
            new = new_out[s, rows, :] + sums[s]
            new_out[s, rows, :] = new
            diffus = diffus + new * new * lookup(diff_table, slot_ids[s])
        diff_out[rows, :] = diffus
        return diffus

    right = even("gx")
    for halo, upper in ((x_a, right), (x_b, jnp.logical_not(right))):
        base = jnp.where(upper, (nx - 1) * ny, 0)
        for part in range(ny // SUB):
            add(
                pl.ds(pl.multiple_of(base + part * SUB, SUB), SUB),
                lambda p, halo=halo, part=part: halo[p, part * SUB : (part + 1) * SUB, :],
            )
    up = even("gy")
    for halo, upper, face in ((y_a, up, face_a), (y_b, jnp.logical_not(up), face_b)):
        rows = pl.ds(jnp.where(upper, ny - 1, 0), nx, stride=ny)
        face[...] = add(rows, lambda p, halo=halo: halo[p])


def chain_ends(source, face):
    one = jnp.ones_like(source[0])

    def sweep(values, faces):
        mass, total, through = one, values[0], one
        for value, f in zip(values[1:], faces):
            share = f / (mass + f)
            total = value + share * total
            mass = 1.0 + share * mass
            through = share * through
        unit = 1.0 / mass
        return total * unit, unit, through * unit

    last, g_last, g_through = sweep(source, face)
    first, g_first, _ = sweep(source[::-1], face[::-1])
    return first, last, g_first, g_through, g_last


def join(left, right):
    first_a, last_a, gff_a, gfl_a, gll_a, d_first, d_last = left
    first_b, last_b, gff_b, gfl_b, gll_b, d_next, d_end = right
    face = 0.5 * (d_last + d_next)
    link = face / (1.0 + face * (gll_a + gff_b))
    flux = link * (first_b - last_a)
    return (
        first_a + flux * gfl_a,
        last_b - flux * gfl_b,
        gff_a - link * gfl_a * gfl_a,
        gfl_a * link * gfl_b,
        gll_b - link * gfl_b * gfl_b,
        d_first,
        d_end,
    )


def fluxes(blocks, flux_left, flux_right):
    count = len(blocks)
    views_left = []
    first, last, gff, gfl, gll, _, d_last = blocks[0]
    view = (last - flux_left * gfl, gll, d_last)
    for m in range(count - 1):
        views_left.append(view)
        if m + 1 < count - 1:
            first, last, gff, gfl, gll, d_first, d_last = blocks[m + 1]
            face = 0.5 * (view[2] + d_first)
            link = face / (1.0 + face * (view[1] + gff))
            flux = link * (first - view[0])
            view = (last - flux * gfl, gll - link * gfl * gfl, d_last)
    views_right = []
    first, last, gff, gfl, gll, d_first, _ = blocks[-1]
    view = (first + flux_right * gfl, gff, d_first)
    for m in range(count - 1, 0, -1):
        views_right.append(view)
        if m - 1 > 0:
            first, last, gff, gfl, gll, d_first, d_last = blocks[m - 1]
            face = 0.5 * (d_last + view[2])
            link = face / (1.0 + face * (gll + view[1]))
            flux = link * (view[0] - last)
            view = (first + flux * gfl, gff - link * gfl * gfl, d_first)
    views_right = views_right[::-1]
    inner = []
    for left, right in zip(views_left, views_right):
        face = 0.5 * (left[2] + right[2])
        inner.append(face * (right[0] - left[0]) / (1.0 + face * (left[1] + right[1])))
    return [flux_left] + inner + [flux_right]


def choose(options, number):
    out = options[0]
    for k in range(1, len(options)):
        out = jnp.where(number == k, options[k], out)
    return out


def members(axis, level, refs):
    stride, radix = level
    own = lax.rem(lax.axis_index(axis) // stride, radix)
    blocks = []
    for m in range(radix):
        number = own ^ m
        blocks.append(tuple(choose([r[q] for r in refs], number) for q in range(7)))
    return own, blocks


def solve_levels(axis, levels, refs):
    position = 0
    groups = []
    for level in levels:
        groups.append(members(axis, level, refs[position : position + level[1]]))
        position += level[1]
    zero = jnp.zeros(refs[0].shape[1:], jnp.float32)
    lower, upper = zero, zero
    for own, blocks in groups[::-1]:
        between = fluxes(blocks, lower, upper)
        lower, upper = choose(between[:-1], own), choose(between[1:], own)
    return lower, upper


def join_kernel(axis, level, *refs):
    out = refs[-1]
    _, blocks = members(axis, level, refs[:-1])
    total = blocks[0]
    for block in blocks[1:]:
        total = join(total, block)
    for q in range(7):
        out[q] = total[q]


def gather_levels(axis, payload, shape):
    count = lax.axis_size(axis)
    levels, refs = [], []
    stride = 1
    while stride < count:
        radix = 2
        level = (stride, radix)
        group = [payload]
        for k in range(1, radix):
            pairs = [(i, i ^ (k * stride)) for i in range(count)]
            group.append(lax.ppermute(payload, axis, pairs))
        levels.append(level)
        refs += group
        stride *= radix
        if stride < count:
            (payload,) = call(
                functools.partial(join_kernel, axis, level), "join_" + axis, [shape], group
            )
    return levels, refs


def flux_x_kernel(shape, diff, conc, y_a, y_b, halo_a, halo_b, payload, source, applied):
    nx, ny, nz = shape
    up = even("gy")
    place = lax.axis_index("gy")
    count = lax.axis_size("gy")
    last = y_a.shape[0] - 1

    def side(a, b, flag):
        return jnp.where(jnp.full((nx, nz), flag.astype(jnp.int32)) == 1, a, b)

    has_low = jnp.where(place > 0, 0.5, 0.0)
    has_high = jnp.where(place < count - 1, 0.5, 0.0)
    d_low = side(halo_b[...], halo_a[...], up)
    d_high = side(halo_a[...], halo_b[...], up)
    c_low = side(y_b[last], y_a[last], up)
    c_high = side(y_a[last], y_b[last], up)
    d_prev, c_prev = diff[pl.ds(0, nx, stride=ny), :], conc[pl.ds(0, nx, stride=ny), :]
    below = has_low * (d_low + d_prev) * (c_prev - c_low)
    for y in range(ny):
        if y + 1 < ny:
            d_next, c_next = diff[pl.ds(y + 1, nx, stride=ny), :], conc[pl.ds(y + 1, nx, stride=ny), :]
            above = 0.5 * (d_prev + d_next) * (c_next - c_prev)
        else:
            d_next, c_next = d_high, c_high
            above = has_high * (d_prev + d_next) * (c_next - c_prev)
        applied[pl.ds(y, nx, stride=ny), :] = above - below
        d_prev, c_prev, below = d_next, c_next, above

    inside = lax.broadcasted_iota(jnp.int32, (ny, nz), 1) < nz - 1
    rows = [slice(x * ny, (x + 1) * ny) for x in range(nx)]
    values, d = [], []
    for x in range(nx):
        here, c = diff[rows[x], :], conc[rows[x], :]
        flux = jnp.where(
            inside, 0.5 * (here + pltpu.roll(here, nz - 1, 1)) * (pltpu.roll(c, nz - 1, 1) - c), 0.0
        )
        value = (c + applied[rows[x], :]) + (flux - pltpu.roll(flux, 1, 1))
        source[rows[x], :] = value
        values.append(value)
        d.append(here)
    face = [0.5 * (a + b) for a, b in zip(d[:-1], d[1:])]
    ends = chain_ends(values, face)
    for q in range(5):
        payload[q] = ends[q]
    payload[5] = d[0]
    payload[6] = d[-1]


def inside_chain(values, face):
    one = jnp.ones_like(face[0])
    mass, total, through = one, values[0], one
    shares, totals, throughs, inverses = [], [], [], []
    for value, f in zip(values[1:], face):
        inverse = 1.0 / (mass + f)
        share = f * inverse
        shares.append(share)
        inverses.append(inverse)
        totals.append(total)
        throughs.append(through)
        total = value + share * total
        mass = 1.0 + share * mass
        through = share * through
    unit = 1.0 / mass
    base, first, last = [total * unit], [through * unit], [unit]
    for share, inverse, total, through in zip(
        shares[::-1], inverses[::-1], totals[::-1], throughs[::-1]
    ):
        base.append(inverse * total + share * base[-1])
        first.append(inverse * through + share * first[-1])
        last.append(share * last[-1])
    return base[::-1], first[::-1], last[::-1]


def inner_x_kernel(shape, diff, source, base_out, first_out, last_out):
    nx, ny, nz = shape
    for part in range(ny // SUB):
        rows = [slice(x * ny + part * SUB, x * ny + (part + 1) * SUB) for x in range(nx)]
        d = [diff[r, :] for r in rows]
        face = [0.5 * (a + b) for a, b in zip(d[:-1], d[1:])]
        base, first, last = inside_chain([source[r, :] for r in rows], face)
        for r, u, f, l in zip(rows, base, first, last):
            base_out[r, :] = u
            first_out[r, :] = f
            last_out[r, :] = l


def flux_y_kernel(shape, levels, diff, base, first, last, applied, *refs):
    nx, ny, nz = shape
    payload, source, section = refs[-3:]
    lower, upper = solve_levels("gx", levels, refs[:-3])
    for x in range(nx):
        r = slice(x * ny, (x + 1) * ny)
        section[r, :] = (base[r, :] + upper * last[r, :] - lower * first[r, :]) - applied[r, :]
    values = [section[pl.ds(y, nx, stride=ny), :] for y in range(ny)]
    d = [diff[pl.ds(y, nx, stride=ny), :] for y in range(ny)]
    for y in range(ny):
        source[y] = values[y]
    face = [0.5 * (a + b) for a, b in zip(d[:-1], d[1:])]
    ends = chain_ends(values, face)
    for q in range(5):
        payload[q] = ends[q]
    payload[5] = d[0]
    payload[6] = d[-1]


def inner_y_kernel(shape, diff, source, base_out, first_out, last_out):
    nx, ny, nz = shape
    d = [diff[pl.ds(y, nx, stride=ny), :] for y in range(ny)]
    face = [0.5 * (a + b) for a, b in zip(d[:-1], d[1:])]
    base, first, last = inside_chain([source[y] for y in range(ny)], face)
    for y in range(ny):
        base_out[y] = base[y]
        first_out[y] = first[y]
        last_out[y] = last[y]


def last_kernel(shape, levels, diff, conc, base, first, last, *refs):
    nx, ny, nz = shape
    out = refs[-1]
    lower, upper = solve_levels("gy", levels, refs[:-1])
    lane = lax.broadcasted_iota(jnp.int32, (nx, nz), 1)
    for y in range(ny):
        rows = pl.ds(y, nx, stride=ny)
        d, c = diff[rows, :], conc[rows, :]
        right = jnp.where(lane < nz - 1, 0.5 * (d + pltpu.roll(d, nz - 1, 1)), 0.0)
        left = pltpu.roll(right, 1, 1)
        flux = right * (pltpu.roll(c, nz - 1, 1) - c)
        value = (base[y] + upper * last[y] - lower * first[y]) - (flux - pltpu.roll(flux, 1, 1))
        mass = jnp.ones((nx, nz), jnp.float32)
        shift = 1
        while True:
            unit = 1.0 / (mass + left + right)
            mass, left, right, value = mass * unit, left * unit, right * unit, value * unit
            value = (
                value + left * pltpu.roll(value, shift, 1) + right * pltpu.roll(value, nz - shift, 1)
            )
            mass = mass + left * pltpu.roll(mass, shift, 1) + right * pltpu.roll(mass, nz - shift, 1)
            if 2 * shift >= nz:
                break
            left = left * pltpu.roll(left, shift, 1)
            right = right * pltpu.roll(right, nz - shift, 1)
            shift *= 2
        out[rows, :] = value / mass


def pair_exchange(axis, first, second):
    count = lax.axis_size(axis)
    near = [(i, i ^ 1) for i in range(count)]
    far = [(i, (i - 1) % count if i % 2 == 0 else (i + 1) % count) for i in range(count)]
    return lax.ppermute(first, axis, near), lax.ppermute(second, axis, far)


def body(phase_frac, phase_ids, conc, pair_class, mobility, drive, diffusivity):
    slots, nx, ny, nz = phase_frac.shape
    phases = drive.shape[0]
    shape = (nx, ny, nz)
    cells = nx * ny
    flat = (cells, nz)
    frac = phase_frac.reshape(slots, cells, nz)
    ids = phase_ids.reshape(slots, cells, nz)
    field = conc.reshape(cells, nz)

    x_a, x_b, y_a, y_b = call(
        functools.partial(faces_kernel, phases, shape),
        "faces",
        [(phases, ny, nz)] * 2 + [(phases + 1, nx, nz)] * 2,
        [frac, ids, field],
    )
    x_a, x_b = pair_exchange("gx", x_a, x_b)
    y_a, y_b = pair_exchange("gy", y_a, y_b)
    count = -(-phases // (nz // phases))
    new, diffus, table = call(
        functools.partial(interior_kernel, phases, shape),
        "interior",
        [(slots, cells, nz), flat, (count * SUB, nz)],
        [frac, ids, field, pair_class, mobility, drive, diffusivity],
        scratch=[(phases, (nx + 2) * (ny + 2 * SUB), nz)],
        scalars=(4, 5, 6),
    )
    new, diffus, face_a, face_b = call(
        functools.partial(outer_kernel, phases, shape),
        "outer",
        [(slots, cells, nz), flat, (nx, nz), (nx, nz)],
        [new, diffus, table, ids, x_a, x_b, y_a, y_b, diffusivity],
        scalars=(8,),
    )
    face_a, face_b = pair_exchange("gy", face_a, face_b)
    payload, source, applied = call(
        functools.partial(flux_x_kernel, shape),
        "flux_x",
        [(7, ny, nz), flat, flat],
        [diffus, field, y_a, y_b, face_a, face_b],
    )
    levels, refs = gather_levels("gx", payload, (7, ny, nz))
    base, first, last = call(
        functools.partial(inner_x_kernel, shape), "inner_x", [flat] * 3, [diffus, source]
    )
    payload, source = call(
        functools.partial(flux_y_kernel, shape, levels),
        "flux_y",
        [(7, nx, nz), (ny, nx, nz)],
        [diffus, base, first, last, applied] + refs,
        scratch=[flat],
    )
    levels, refs = gather_levels("gy", payload, (7, nx, nz))
    base, first, last = call(
        functools.partial(inner_y_kernel, shape), "inner_y", [(ny, nx, nz)] * 3, [diffus, source]
    )
    (out,) = call(
        functools.partial(last_kernel, shape, levels),
        "last",
        [flat],
        [diffus, field, base, first, last] + refs,
    )
    return new.reshape(slots, nx, ny, nz), out.reshape(nx, ny, nz)


def solution(mesh):
    split = P(None, "gx", "gy", None)
    return jax.shard_map(
        body,
        mesh=mesh,
        in_specs=(split, split, P("gx", "gy", None), P(), P(), P(), P()),
        out_specs=(split, P("gx", "gy", None)),
        check_vma=False,
    )
```

```python
import functools

import jax
import jax.numpy as jnp
from jax import lax
from jax.experimental import pallas as pl
from jax.experimental.pallas import tpu as pltpu
from jax.sharding import PartitionSpec as P

KAPPA = 2.0
DRIVE = 4.0
SUB = 8

VMEM = pl.BlockSpec(memory_space=pltpu.VMEM)
SMEM = pl.BlockSpec(memory_space=pltpu.SMEM)
HBM = pl.BlockSpec(memory_space=pltpu.HBM)


def call(kernel, name, outs, ins, scratch=(), aliases={}, cost=20000, scalars=(), far=()):
    f32 = jnp.float32
    place = [SMEM if i in scalars else HBM if i in far else VMEM for i in range(len(ins))]
    return pl.pallas_call(
        kernel,
        name=name,
        out_shape=[s if isinstance(s, jax.ShapeDtypeStruct) else jax.ShapeDtypeStruct(s, f32) for s in outs],
        in_specs=place,
        out_specs=[VMEM] * len(outs),
        scratch_shapes=[pltpu.VMEM(s, f32) if isinstance(s, tuple) else s for s in scratch],
        input_output_aliases=aliases,
        compiler_params=pltpu.CompilerParams(vmem_limit_bytes=12 << 20),
        cost_estimate=pl.CostEstimate(flops=cost * 1000, bytes_accessed=1 << 20, transcendentals=0),
    )(*ins)


def far_away(array):
    return pltpu.with_memory_space_constraint(array, pltpu.HBM)


def lookup(table, index):
    dims = lax.GatherDimensionNumbers(
        offset_dims=(),
        collapsed_slice_dims=(1,),
        start_index_map=(1,),
        operand_batching_dims=(0,),
        start_indices_batching_dims=(0,),
    )
    return lax.gather(
        table, index[..., None], dims, (1, 1), mode=lax.GatherScatterMode.PROMISE_IN_BOUNDS
    )


def scalar_table(ref, shape):
    lane = lax.broadcasted_iota(jnp.int32, shape, 1)
    table = jnp.zeros(shape, jnp.float32)
    for k in range(ref.shape[0]):
        table = jnp.where(lane == k, ref[k], table)
    return table


def even(axis):
    return lax.rem(lax.axis_index(axis), 2) == 0


def pick_rows(ids, fields, count):
    rows = []
    for phase in range(count):
        total = jnp.zeros(fields[0].shape, jnp.float32)
        for slot_id, field in zip(ids, fields):
            total = jnp.where(slot_id == phase, field, total)
        rows.append(total)
    return rows


def pick_slots(ids, rows):
    picked = [jnp.zeros(ids[0].shape, jnp.float32) for _ in ids]
    for phase, row in enumerate(rows):
        picked = [jnp.where(i == phase, row, t) for i, t in zip(ids, picked)]
    return picked


def exchange(level, ids, tables, phases, source=None):
    width = tables.shape[1]
    per_row = width // phases
    count = tables.shape[0] // SUB
    lane_of = [lax.rem(i, per_row) * phases if per_row & (per_row - 1) else (i & (per_row - 1)) * phases for i in ids]
    sums = [jnp.zeros(level[0].shape, jnp.float32) for _ in level]
    for a in range(len(level)):
        above = [ids[a] >= t * per_row for t in range(1, count)]
        for b in range(a + 1, len(level)):
            index = lane_of[a] + ids[b]
            mob = lookup(tables[0:SUB], index)
            for t in range(1, count):
                mob = jnp.where(above[t - 1], lookup(tables[t * SUB : (t + 1) * SUB], index), mob)
            term = level[a] - level[b]
            if source is not None:
                frac, drive, conc = source
                term = term + (conc * frac[a]) * (frac[b] * (drive[a] - drive[b]))
            term = mob * term
            sums[a] = sums[a] + term
            sums[b] = sums[b] - term
    return sums


def faces_kernel(phases, shape, frac_far, ids_far, conc_far, frac, ids, conc, x_a, x_b, y_a, y_b, sems):
    nx, ny, _ = shape
    slots = frac.shape[0]
    half = slots // 2
    copies = []
    for k, (far, near) in enumerate(
        [
            (frac_far.at[:half], frac.at[:half]),
            (ids_far.at[:half], ids.at[:half]),
            (frac_far.at[half:], frac.at[half:]),
            (ids_far.at[half:], ids.at[half:]),
            (conc_far, conc),
        ]
    ):
        copies.append(pltpu.make_async_copy(far, near, sems.at[k]))
        copies[-1].start()
    for copy in copies:
        copy.wait()
    right = even("gx")
    for out, upper in ((x_a, right), (x_b, jnp.logical_not(right))):
        base = jnp.where(upper, (nx - 1) * ny, 0)
        for part in range(ny // SUB):
            rows = pl.ds(pl.multiple_of(base + part * SUB, SUB), SUB)
            held = pick_rows(
                [ids[s, rows, :] for s in range(slots)],
                [frac[s, rows, :] for s in range(slots)],
                phases,
            )
            for phase in range(phases):
                out[phase, part * SUB : (part + 1) * SUB, :] = held[phase]
    up = even("gy")
    for out, upper in ((y_a, up), (y_b, jnp.logical_not(up))):
        rows = pl.ds(jnp.where(upper, ny - 1, 0), nx, stride=ny)
        held = pick_rows(
            [ids[s, rows, :] for s in range(slots)],
            [frac[s, rows, :] for s in range(slots)],
            phases,
        )
        for phase in range(phases):
            out[phase] = held[phase]
        out[phases] = conc[rows, :]


def interior_kernel(
    phases, shape, frac, ids, conc, *rest
):
    new_out, diff_out, table_out, diff_table_out, dense, pair_class, mobility, drive, diffusivity, sems = rest[4:]
    copies = [
        pltpu.make_async_copy(far, near, sems.at[k])
        for k, (far, near) in enumerate(zip(rest[:4], (pair_class, mobility, drive, diffusivity)))
    ]
    for copy in copies:
        copy.start()
    nx, ny, nz = shape
    slots = frac.shape[0]
    pitch = ny + 2 * SUB
    parts = ny // SUB
    per_row = nz // phases
    count = -(-phases // per_row)
    nothing = jnp.zeros((SUB, nz), jnp.float32)

    def clear(phase, carry):
        for plane in range(nx + 2):
            for part in range(parts + 2):
                if plane in (0, nx + 1) or part in (0, parts + 1):
                    dense[phase, plane * pitch + part * SUB : plane * pitch + (part + 1) * SUB, :] = nothing
        return carry

    lax.fori_loop(0, phases, clear, 0)

    def build(x, carry):
        for part in range(parts):
            rows = pl.ds(pl.multiple_of(x * ny, SUB) + part * SUB, SUB)
            held = pick_rows(
                [ids[s, rows, :] for s in range(slots)],
                [frac[s, rows, :] for s in range(slots)],
                phases,
            )
            into = pl.ds(pl.multiple_of((x + 1) * pitch, SUB) + (part + 1) * SUB, SUB)
            for phase in range(phases):
                dense[phase, into, :] = held[phase]
        return carry

    lax.fori_loop(0, nx, build, 0)
    for copy in copies:
        copy.wait()
    lane = lax.broadcasted_iota(jnp.int32, (per_row, nz), 1)
    row = lax.broadcasted_iota(jnp.int32, (per_row, nz), 0)
    for t in range(count):
        block = pair_class[t * per_row : (t + 1) * per_row, :]
        wide = jnp.concatenate([block] * per_row, axis=1)
        values = jnp.zeros(wide.shape, jnp.float32)
        for k in range(mobility.shape[0]):
            values = jnp.where(wide == k, mobility[k], values)
        line = jnp.sum(
            jnp.where((lane >= row * phases) & (lane < (row + 1) * phases), values, 0.0),
            axis=0,
            keepdims=True,
        )
        table_out[t * SUB : (t + 1) * SUB, :] = jnp.broadcast_to(line, (SUB, nz))
    drive_table = scalar_table(drive, (SUB, nz))
    diff_table = scalar_table(diffusivity, (SUB, nz))
    diff_table_out[...] = diff_table

    def update(x, carry):
        for part in range(parts):
            rows = pl.ds(pl.multiple_of(x * ny, SUB) + part * SUB, SUB)
            at = pl.multiple_of((x + 1) * pitch, SUB) + (part + 1) * SUB

            def laplacian():
                for phase in range(phases):
                    centre = dense[phase, pl.ds(at, SUB), :]
                    along_x = dense[phase, pl.ds(at + pitch, SUB), :] + dense[phase, pl.ds(at - pitch, SUB), :]
                    along_y = dense[phase, pl.ds(at + 1, SUB), :] + dense[phase, pl.ds(at - 1, SUB), :]
                    along_z = pltpu.roll(centre, nz - 1, 1) + pltpu.roll(centre, 1, 1)
                    yield (along_x + along_y + along_z) - 6.0 * centre

            slot_ids = [ids[s, rows, :] for s in range(slots)]
            curvature = pick_slots(slot_ids, laplacian())
            slot_frac = [frac[s, rows, :] for s in range(slots)]
            level = [c + KAPPA * f for c, f in zip(curvature, slot_frac)]
            slot_drive = [lookup(drive_table, i) for i in slot_ids]
            sums = exchange(
                level, slot_ids, table_out, phases, (slot_frac, slot_drive, DRIVE * conc[rows, :])
            )
            diffus = jnp.ones((SUB, nz), jnp.float32)
            for s in range(slots):
                new = slot_frac[s] + sums[s]
                new_out[s, rows, :] = new
                diffus = diffus + new * new * lookup(diff_table, slot_ids[s])
            diff_out[rows, :] = diffus
        return carry

    lax.fori_loop(0, nx, update, 0)


def outer_kernel(
    phases, shape, new_in, diff_in, table, ids, x_a, x_b, y_a, y_b, diff_table_in,
    new_out, diff_out, face_a, face_b,
):
    nx, ny, nz = shape
    slots = new_in.shape[0]
    diff_table = diff_table_in[...]
    del new_in, diff_in

    def add(rows, halo):
        slot_ids = [ids[s, rows, :] for s in range(slots)]
        level = pick_slots(slot_ids, (halo(p) for p in range(phases)))
        sums = exchange(level, slot_ids, table, phases)
        diffus = jnp.ones(sums[0].shape, jnp.float32)
        for s in range(slots):
            new = new_out[s, rows, :] + sums[s]
            new_out[s, rows, :] = new
            diffus = diffus + new * new * lookup(diff_table, slot_ids[s])
        diff_out[rows, :] = diffus
        return diffus

    right = even("gx")
    for halo, upper in ((x_a, right), (x_b, jnp.logical_not(right))):
        base = jnp.where(upper, (nx - 1) * ny, 0)
        for part in range(ny // SUB):
            add(
                pl.ds(pl.multiple_of(base + part * SUB, SUB), SUB),
                lambda p, halo=halo, part=part: halo[p, part * SUB : (part + 1) * SUB, :],
            )
    up = even("gy")
    for halo, upper, face in ((y_a, up, face_a), (y_b, jnp.logical_not(up), face_b)):
        rows = pl.ds(jnp.where(upper, ny - 1, 0), nx, stride=ny)
        face[...] = add(rows, lambda p, halo=halo: halo[p])


def chain_ends(source, face):
    one = jnp.ones_like(source[0])

    def sweep(values, faces):
        mass, total, through = one, values[0], one
        for value, f in zip(values[1:], faces):
            share = f / (mass + f)
            total = value + share * total
            mass = 1.0 + share * mass
            through = share * through
        unit = 1.0 / mass
        return total * unit, unit, through * unit

    last, g_last, g_through = sweep(source, face)
    first, g_first, _ = sweep(source[::-1], face[::-1])
    return first, last, g_first, g_through, g_last


def join(left, right):
    first_a, last_a, gff_a, gfl_a, gll_a, d_first, d_last = left
    first_b, last_b, gff_b, gfl_b, gll_b, d_next, d_end = right
    face = 0.5 * (d_last + d_next)
    link = face / (1.0 + face * (gll_a + gff_b))
    flux = link * (first_b - last_a)
    return (
        first_a + flux * gfl_a,
        last_b - flux * gfl_b,
        gff_a - link * gfl_a * gfl_a,
        gfl_a * link * gfl_b,
        gll_b - link * gfl_b * gfl_b,
        d_first,
        d_end,
    )


def fluxes(blocks, flux_left, flux_right):
    count = len(blocks)
    views_left = []
    first, last, gff, gfl, gll, _, d_last = blocks[0]
    view = (last - flux_left * gfl, gll, d_last)
    for m in range(count - 1):
        views_left.append(view)
        if m + 1 < count - 1:
            first, last, gff, gfl, gll, d_first, d_last = blocks[m + 1]
            face = 0.5 * (view[2] + d_first)
            link = face / (1.0 + face * (view[1] + gff))
            flux = link * (first - view[0])
            view = (last - flux * gfl, gll - link * gfl * gfl, d_last)
    views_right = []
    first, last, gff, gfl, gll, d_first, _ = blocks[-1]
    view = (first + flux_right * gfl, gff, d_first)
    for m in range(count - 1, 0, -1):
        views_right.append(view)
        if m - 1 > 0:
            first, last, gff, gfl, gll, d_first, d_last = blocks[m - 1]
            face = 0.5 * (d_last + view[2])
            link = face / (1.0 + face * (gll + view[1]))
            flux = link * (view[0] - last)
            view = (first + flux * gfl, gff - link * gfl * gfl, d_first)
    views_right = views_right[::-1]
    inner = []
    for left, right in zip(views_left, views_right):
        face = 0.5 * (left[2] + right[2])
        inner.append(face * (right[0] - left[0]) / (1.0 + face * (left[1] + right[1])))
    return [flux_left] + inner + [flux_right]


def choose(options, number):
    out = options[0]
    for k in range(1, len(options)):
        out = jnp.where(number == k, options[k], out)
    return out


def members(axis, level, refs):
    stride, radix = level
    own = lax.rem(lax.axis_index(axis) // stride, radix)
    blocks = []
    for m in range(radix):
        number = own ^ m
        blocks.append(tuple(choose([r[q] for r in refs], number) for q in range(7)))
    return own, blocks


def solve_levels(axis, levels, refs):
    position = 0
    groups = []
    for level in levels:
        groups.append(members(axis, level, refs[position : position + level[1]]))
        position += level[1]
    zero = jnp.zeros(refs[0].shape[1:], jnp.float32)
    lower, upper = zero, zero
    for own, blocks in groups[::-1]:
        between = fluxes(blocks, lower, upper)
        lower, upper = choose(between[:-1], own), choose(between[1:], own)
    return lower, upper


def join_kernel(axis, level, *refs):
    out = refs[-1]
    _, blocks = members(axis, level, refs[:-1])
    total = blocks[0]
    for block in blocks[1:]:
        total = join(total, block)
    for q in range(7):
        out[q] = total[q]


def gather_levels(axis, payload, shape):
    count = lax.axis_size(axis)
    levels, refs = [], []
    stride = 1
    while stride < count:
        radix = 2
        level = (stride, radix)
        group = [payload]
        for k in range(1, radix):
            pairs = [(i, i ^ (k * stride)) for i in range(count)]
            group.append(lax.ppermute(payload, axis, pairs))
        levels.append(level)
        refs += group
        stride *= radix
        if stride < count:
            (payload,) = call(
                functools.partial(join_kernel, axis, level), "join_" + axis, [shape], group
            )
    return levels, refs


def flux_x_kernel(shape, diff, conc, y_a, y_b, halo_a, halo_b, _, payload, source, applied):
    nx, ny, nz = shape
    up = even("gy")
    place = lax.axis_index("gy")
    count = lax.axis_size("gy")
    last = y_a.shape[0] - 1

    def side(a, b, flag):
        return jnp.where(jnp.full((nx, nz), flag.astype(jnp.int32)) == 1, a, b)

    has_low = jnp.where(place > 0, 0.5, 0.0)
    has_high = jnp.where(place < count - 1, 0.5, 0.0)
    d_low = side(halo_b[...], halo_a[...], up)
    d_high = side(halo_a[...], halo_b[...], up)
    c_low = side(y_b[last], y_a[last], up)
    c_high = side(y_a[last], y_b[last], up)
    d_prev, c_prev = diff[pl.ds(0, nx, stride=ny), :], conc[pl.ds(0, nx, stride=ny), :]
    below = has_low * (d_low + d_prev) * (c_prev - c_low)
    for y in range(ny):
        if y + 1 < ny:
            d_next, c_next = diff[pl.ds(y + 1, nx, stride=ny), :], conc[pl.ds(y + 1, nx, stride=ny), :]
            above = 0.5 * (d_prev + d_next) * (c_next - c_prev)
        else:
            d_next, c_next = d_high, c_high
            above = has_high * (d_prev + d_next) * (c_next - c_prev)
        applied[pl.ds(y, nx, stride=ny), :] = above - below
        d_prev, c_prev, below = d_next, c_next, above

    inside = lax.broadcasted_iota(jnp.int32, (ny, nz), 1) < nz - 1
    rows = [slice(x * ny, (x + 1) * ny) for x in range(nx)]
    values, d = [], []
    for x in range(nx):
        here, c = diff[rows[x], :], conc[rows[x], :]
        flux = jnp.where(
            inside, 0.5 * (here + pltpu.roll(here, nz - 1, 1)) * (pltpu.roll(c, nz - 1, 1) - c), 0.0
        )
        value = (c + applied[rows[x], :]) + (flux - pltpu.roll(flux, 1, 1))
        source[rows[x], :] = value
        values.append(value)
        d.append(here)
    face = [0.5 * (a + b) for a, b in zip(d[:-1], d[1:])]
    ends = chain_ends(values, face)
    for q in range(5):
        payload[q] = ends[q]
    payload[5] = d[0]
    payload[6] = d[-1]


def inside_chain(values, face):
    one = jnp.ones_like(face[0])
    mass, total, through = one, values[0], one
    shares, totals, throughs, inverses = [], [], [], []
    for value, f in zip(values[1:], face):
        inverse = 1.0 / (mass + f)
        share = f * inverse
        shares.append(share)
        inverses.append(inverse)
        totals.append(total)
        throughs.append(through)
        total = value + share * total
        mass = 1.0 + share * mass
        through = share * through
    unit = 1.0 / mass
    base, first, last = [total * unit], [through * unit], [unit]
    for share, inverse, total, through in zip(
        shares[::-1], inverses[::-1], totals[::-1], throughs[::-1]
    ):
        base.append(inverse * total + share * base[-1])
        first.append(inverse * through + share * first[-1])
        last.append(share * last[-1])
    return base[::-1], first[::-1], last[::-1]


def inner_x_kernel(shape, diff, source, base_out, first_out, last_out):
    nx, ny, nz = shape
    for part in range(ny // SUB):
        rows = [slice(x * ny + part * SUB, x * ny + (part + 1) * SUB) for x in range(nx)]
        d = [diff[r, :] for r in rows]
        face = [0.5 * (a + b) for a, b in zip(d[:-1], d[1:])]
        base, first, last = inside_chain([source[r, :] for r in rows], face)
        for r, u, f, l in zip(rows, base, first, last):
            base_out[r, :] = u
            first_out[r, :] = f
            last_out[r, :] = l


def flux_y_kernel(shape, levels, diff, base, first, last, applied, _, *refs):
    nx, ny, nz = shape
    payload, source, section = refs[-3:]
    lower, upper = solve_levels("gx", levels, refs[:-3])
    for x in range(nx):
        r = slice(x * ny, (x + 1) * ny)
        section[r, :] = (base[r, :] + upper * last[r, :] - lower * first[r, :]) - applied[r, :]
    values = [section[pl.ds(y, nx, stride=ny), :] for y in range(ny)]
    d = [diff[pl.ds(y, nx, stride=ny), :] for y in range(ny)]
    for y in range(ny):
        source[y] = values[y]
    face = [0.5 * (a + b) for a, b in zip(d[:-1], d[1:])]
    ends = chain_ends(values, face)
    for q in range(5):
        payload[q] = ends[q]
    payload[5] = d[0]
    payload[6] = d[-1]


def inner_y_kernel(shape, diff, source, base_out, first_out, last_out):
    nx, ny, nz = shape
    d = [diff[pl.ds(y, nx, stride=ny), :] for y in range(ny)]
    face = [0.5 * (a + b) for a, b in zip(d[:-1], d[1:])]
    base, first, last = inside_chain([source[y] for y in range(ny)], face)
    for y in range(ny):
        base_out[y] = base[y]
        first_out[y] = first[y]
        last_out[y] = last[y]


def steps_of(nz):
    count = 1
    while 2**count < nz:
        count += 1
    return count


def coefficients_z_kernel(shape, diff, conc, applied, start, left_out, right_out, unit_out):
    nx, ny, nz = shape
    lane = lax.broadcasted_iota(jnp.int32, (nx, nz), 1)

    state = []
    for y in range(ny):
        rows = pl.ds(y, nx, stride=ny)
        d, c = diff[rows, :], conc[rows, :]
        right = jnp.where(lane < nz - 1, 0.5 * (d + pltpu.roll(d, nz - 1, 1)), 0.0)
        left = pltpu.roll(right, 1, 1)
        flux = right * (pltpu.roll(c, nz - 1, 1) - c)
        applied[y] = flux - pltpu.roll(flux, 1, 1)
        mass = jnp.ones((nx, nz), jnp.float32)
        unit = 1.0 / (mass + left + right)
        start[y] = unit
        state.append((mass, left, right, unit))
    for step in range(steps_of(nz)):
        shift = 2**step
        for y in range(ny):
            mass, left, right, unit = state[y]
            mass, left, right = mass * unit, left * unit, right * unit
            mass = mass + left * pltpu.roll(mass, shift, 1) + right * pltpu.roll(mass, nz - shift, 1)
            wide_left = left * pltpu.roll(left, shift, 1)
            wide_right = right * pltpu.roll(right, nz - shift, 1)
            unit = 1.0 / (mass + wide_left + wide_right) if 2 * shift < nz else 1.0 / mass
            left_out[step, y] = left * unit
            right_out[step, y] = right * unit
            unit_out[step, y] = unit
            state[y] = mass, wide_left, wide_right, unit


def last_kernel(shape, levels, applied, start, left, right, unit, base, first, last, *refs):
    nx, ny, nz = shape
    out = refs[-1]
    lower, upper = solve_levels("gy", levels, refs[:-1])
    values = [
        ((base[y] + upper * last[y] - lower * first[y]) - applied[y]) * start[y] for y in range(ny)
    ]
    for step in range(steps_of(nz)):
        shift = 2**step
        values = [
            unit[step, y] * v
            + left[step, y] * pltpu.roll(v, shift, 1)
            + right[step, y] * pltpu.roll(v, nz - shift, 1)
            for y, v in enumerate(values)
        ]
    for y in range(ny):
        out[pl.ds(y, nx, stride=ny), :] = values[y]


def commit_kernel(new, out, sem):
    copy = pltpu.make_async_copy(new, out, sem)
    copy.start()
    copy.wait()


def pair_exchange(axis, first, second):
    count = lax.axis_size(axis)
    near = [(i, i ^ 1) for i in range(count)]
    far = [(i, (i - 1) % count if i % 2 == 0 else (i + 1) % count) for i in range(count)]
    return lax.ppermute(first, axis, near), lax.ppermute(second, axis, far)


def body(phase_frac, phase_ids, conc, pair_class, mobility, drive, diffusivity):
    slots, nx, ny, nz = phase_frac.shape
    phases = drive.shape[0]
    shape = (nx, ny, nz)
    cells = nx * ny
    flat = (cells, nz)
    frac = far_away(phase_frac.reshape(slots, cells, nz))
    ids = far_away(phase_ids.reshape(slots, cells, nz))
    field = far_away(conc.reshape(cells, nz))

    frac, ids, field, x_a, x_b, y_a, y_b = call(
        functools.partial(faces_kernel, phases, shape),
        "faces",
        [frac.shape, jax.ShapeDtypeStruct(ids.shape, ids.dtype), flat]
        + [(phases, ny, nz)] * 2
        + [(phases + 1, nx, nz)] * 2,
        [frac, ids, field],
        scratch=[pltpu.SemaphoreType.DMA((5,))],
        far=(0, 1, 2),
    )
    x_a, x_b = pair_exchange("gx", x_a, x_b)
    y_a, y_b = pair_exchange("gy", y_a, y_b)
    count = -(-phases // (nz // phases))
    small = [pair_class, mobility, drive, diffusivity]
    new, diffus, table, diff_table = call(
        functools.partial(interior_kernel, phases, shape),
        "interior",
        [(slots, cells, nz), flat, (count * SUB, nz), (SUB, nz)],
        [frac, ids, field] + [far_away(v) for v in small],
        scratch=[
            (phases, (nx + 2) * (ny + 2 * SUB), nz),
            pltpu.VMEM(pair_class.shape, pair_class.dtype),
        ]
        + [pltpu.SMEM(v.shape, v.dtype) for v in small[1:]]
        + [pltpu.SemaphoreType.DMA((4,))],
        far=(3, 4, 5, 6),
    )
    new, diffus, face_a, face_b = call(
        functools.partial(outer_kernel, phases, shape),
        "outer",
        [(slots, cells, nz), flat, (nx, nz), (nx, nz)],
        [new, diffus, table, ids, x_a, x_b, y_a, y_b, diff_table],
        aliases={0: 0, 1: 1},
    )
    face_a, face_b = pair_exchange("gy", face_a, face_b)
    (new,) = pl.pallas_call(
        commit_kernel,
        name="commit",
        out_shape=[jax.ShapeDtypeStruct(new.shape, new.dtype)],
        in_specs=[VMEM],
        out_specs=[HBM],
        scratch_shapes=[pltpu.SemaphoreType.DMA],
        compiler_params=pltpu.CompilerParams(vmem_limit_bytes=12 << 20),
        cost_estimate=pl.CostEstimate(flops=20000000, bytes_accessed=1 << 20, transcendentals=0),
    )(new)
    payload, source, applied = call(
        functools.partial(flux_x_kernel, shape),
        "flux_x",
        [(7, ny, nz), flat, flat],
        [diffus, field, y_a, y_b, face_a, face_b, far_away(new)],
        far=(6,),
    )
    levels, refs = gather_levels("gx", payload, (7, ny, nz))
    applied_z, start, left, right, unit = call(
        functools.partial(coefficients_z_kernel, shape),
        "coefficients_z",
        [(ny, nx, nz)] * 2 + [(steps_of(nz), ny, nx, nz)] * 3,
        [diffus, field],
    )
    base, first, last = call(
        functools.partial(inner_x_kernel, shape), "inner_x", [flat] * 3, [diffus, source]
    )
    payload, source = call(
        functools.partial(flux_y_kernel, shape, levels),
        "flux_y",
        [(7, nx, nz), (ny, nx, nz)],
        [diffus, base, first, last, applied, applied_z] + refs,
        scratch=[flat],
    )
    levels, refs = gather_levels("gy", payload, (7, nx, nz))
    base, first, last = call(
        functools.partial(inner_y_kernel, shape), "inner_y", [(ny, nx, nz)] * 3, [diffus, source]
    )
    (out,) = call(
        functools.partial(last_kernel, shape, levels),
        "last",
        [flat],
        [applied_z, start, left, right, unit, base, first, last] + refs,
    )
    return new.reshape(slots, nx, ny, nz), out.reshape(nx, ny, nz)


def solution(mesh):
    split = P(None, "gx", "gy", None)
    return jax.shard_map(
        body,
        mesh=mesh,
        in_specs=(split, split, P("gx", "gy", None), P(), P(), P(), P()),
        out_specs=(split, P("gx", "gy", None)),
        check_vma=False,
    )
```

```python
import functools

import jax
import jax.numpy as jnp
from jax import lax
from jax.experimental import pallas as pl
from jax.experimental.pallas import tpu as pltpu
from jax.sharding import PartitionSpec as P

KAPPA = 2.0
DRIVE = 4.0
SUB = 8

VMEM = pl.BlockSpec(memory_space=pltpu.VMEM)
SMEM = pl.BlockSpec(memory_space=pltpu.SMEM)
HBM = pl.BlockSpec(memory_space=pltpu.HBM)


def call(kernel, name, outs, ins, scratch=(), aliases={}, cost=20000, scalars=(), far=()):
    f32 = jnp.float32
    place = [SMEM if i in scalars else HBM if i in far else VMEM for i in range(len(ins))]
    return pl.pallas_call(
        kernel,
        name=name,
        out_shape=[s if isinstance(s, jax.ShapeDtypeStruct) else jax.ShapeDtypeStruct(s, f32) for s in outs],
        in_specs=place,
        out_specs=[VMEM] * len(outs),
        scratch_shapes=[pltpu.VMEM(s, f32) if isinstance(s, tuple) else s for s in scratch],
        input_output_aliases=aliases,
        compiler_params=pltpu.CompilerParams(vmem_limit_bytes=12 << 20),
        cost_estimate=pl.CostEstimate(flops=cost * 1000, bytes_accessed=1 << 20, transcendentals=0),
    )(*ins)


def far_away(array):
    return pltpu.with_memory_space_constraint(array, pltpu.HBM)


def lookup(table, index):
    dims = lax.GatherDimensionNumbers(
        offset_dims=(),
        collapsed_slice_dims=(1,),
        start_index_map=(1,),
        operand_batching_dims=(0,),
        start_indices_batching_dims=(0,),
    )
    return lax.gather(
        table, index[..., None], dims, (1, 1), mode=lax.GatherScatterMode.PROMISE_IN_BOUNDS
    )


def lane_table(ref, nz):
    row = jnp.concatenate([ref[...]] * (nz // ref.shape[1]), axis=1)
    return jnp.broadcast_to(row, (SUB, nz))


def even(axis):
    return lax.rem(lax.axis_index(axis), 2) == 0


def pick_rows(ids, fields, count):
    rows = []
    for phase in range(count):
        total = jnp.zeros(fields[0].shape, jnp.float32)
        for slot_id, field in zip(ids, fields):
            total = jnp.where(slot_id == phase, field, total)
        rows.append(total)
    return rows


def pick_slots(ids, rows):
    rows = list(rows)
    bits = range((len(rows) - 1).bit_length())
    picked = []
    for slot_id in ids:
        level = rows
        for bit in bits:
            odd = (slot_id & (1 << bit)) != 0
            level = [
                jnp.where(odd, level[k + 1], level[k]) if k + 1 < len(level) else level[k]
                for k in range(0, len(level), 2)
            ]
        picked.append(level[0])
    return picked


def pair_base(phase, phases):
    return phase * (2 * phases - 3 - phase) // 2 - 1


def pair_table(pair_class, mobility, phases, nz):
    wide = jnp.concatenate([pair_class[...]] * (nz // phases), axis=1)
    options = lane_table(mobility, nz)
    values = jnp.concatenate(
        [lookup(options, wide[k : k + SUB]) for k in range(0, phases, SUB)], axis=0
    )
    lane = lax.broadcasted_iota(jnp.int32, (SUB, nz), 1)
    table = jnp.zeros((SUB, nz), jnp.float32)
    for p in range(phases - 1):
        base = pair_base(p, phases)
        row = jnp.broadcast_to(values[p : p + 1, :], (SUB, nz))
        shift = base % phases
        if shift:
            row = pltpu.roll(row, shift, 1)
        table = jnp.where((lane > base + p) & (lane < base + phases), row, table)
    return table


def pairs_of(count):
    return [(a, b) for a in range(count) for b in range(a + 1, count)]


def mobilities(ids, table, phases):
    base = [lax.shift_right_arithmetic(i * (2 * phases - 3 - i), 1) - 1 for i in ids]
    return [
        lookup(table, jnp.minimum(base[a], base[b]) + jnp.maximum(ids[a], ids[b]))
        for a, b in pairs_of(len(ids))
    ]


def exchange(level, mobs, source=None):
    sums = [jnp.zeros(level[0].shape, jnp.float32) for _ in level]
    for (a, b), mob in zip(pairs_of(len(level)), mobs):
        term = level[a] - level[b]
        if source is not None:
            pulled, frac, drive = source
            term = term + pulled[a] * (frac[b] * (drive[a] - drive[b]))
        term = mob * term
        sums[a] = sums[a] + term
        sums[b] = sums[b] - term
    return sums


def plane_rows(shape, upper):
    nx, ny, _ = shape
    return pl.ds(pl.multiple_of(jnp.where(upper, (nx - 1) * ny, 0), SUB), ny)


def first_kernel(phases, shape, *refs):
    nx, ny, nz = shape
    count = (len(refs) - 5) // 2
    far, near, outs, held_far, sems = refs[:count], refs[count:-5], refs[-5:-3], refs[-3:-1], refs[-1]
    right = even("gx")
    copies = []
    for k, upper in enumerate((right, jnp.logical_not(right))):
        rows = plane_rows(shape, upper)
        for source, target in zip(far[:2], held_far):
            copies.append(
                pltpu.make_async_copy(source.at[:, rows, :], target.at[k], sems.at[len(copies)])
            )
    for source, target in zip(far, near):
        half = source.shape[0] // 2 if len(source.shape) == 3 else 0
        for piece in ([slice(0, half), slice(half, None)] if half else [slice(None)]):
            copies.append(
                pltpu.make_async_copy(source.at[piece], target.at[piece], sems.at[len(copies)])
            )
    for copy in copies:
        copy.start()
    frac, ids = held_far
    slots = frac.shape[1]
    for k, out in enumerate(outs):
        for copy in copies[2 * k : 2 * k + 2]:
            copy.wait()
        for part in range(ny // SUB):
            rows = slice(part * SUB, (part + 1) * SUB)
            held = pick_rows(
                [ids[k, s, rows, :] for s in range(slots)],
                [frac[k, s, rows, :] for s in range(slots)],
                phases,
            )
            for phase in range(phases):
                out[phase, rows, :] = held[phase]
    for copy in copies[4:]:
        copy.wait()


def faces_kernel(phases, shape, frac, ids, conc, y_a, y_b):
    nx, ny, _ = shape
    slots = frac.shape[0]
    up = even("gy")
    for out, upper in ((y_b, jnp.logical_not(up)), (y_a, up)):
        rows = pl.ds(jnp.where(upper, ny - 1, 0), nx, stride=ny)
        held = pick_rows(
            [ids[s, rows, :] for s in range(slots)],
            [frac[s, rows, :] for s in range(slots)],
            phases,
        )
        for phase in range(phases):
            out[phase] = held[phase]
        out[phases] = conc[rows, :]


def build_kernel(phases, shape, frac, ids, pair_class, mobility, dense, mob_out):
    nx, ny, nz = shape
    slots = frac.shape[0]
    pitch = ny + 2 * SUB
    parts = ny // SUB
    table = pair_table(pair_class, mobility, phases, nz)
    nothing = jnp.zeros((SUB, nz), jnp.float32)

    def clear(phase, carry):
        for plane in range(nx + 2):
            for part in range(parts + 2):
                if plane in (0, nx + 1) or part in (0, parts + 1):
                    at = plane * pitch + part * SUB
                    dense[phase, at : at + SUB, :] = nothing
        return carry

    lax.fori_loop(0, phases, clear, 0)

    def build(x, carry):
        for part in range(parts):
            rows = pl.ds(pl.multiple_of(x * ny, SUB) + part * SUB, SUB)
            slot_ids = [ids[s, rows, :] for s in range(slots)]
            for k, mob in enumerate(mobilities(slot_ids, table, phases)):
                mob_out[k, rows, :] = mob
            held = pick_rows(slot_ids, [frac[s, rows, :] for s in range(slots)], phases)
            into = pl.ds(pl.multiple_of((x + 1) * pitch, SUB) + (part + 1) * SUB, SUB)
            for phase in range(phases):
                dense[phase, into, :] = held[phase]
        return carry

    lax.fori_loop(0, nx, build, 0, unroll=2 if nx % 2 == 0 else 1)


def tables_of(phases, drive, diffusivity, nz):
    return lane_table(drive, nz), lane_table(diffusivity, nz)


def renew(laplacian, rows, mobs, frac, ids, conc, tables):
    slots = frac.shape[0]
    slot_ids = [ids[s, rows, :] for s in range(slots)]
    slot_drive, slot_diff = [], []
    for i in slot_ids:
        slot_drive.append(lookup(tables[0], i))
        slot_diff.append(lookup(tables[1], i))
    curvature = pick_slots(slot_ids, laplacian)
    slot_frac = [frac[s, rows, :] for s in range(slots)]
    level = [c + KAPPA * f for c, f in zip(curvature, slot_frac)]
    scaled = DRIVE * conc[rows, :]
    pulled = [scaled * f for f in slot_frac]
    sums = exchange(
        level, [mobs[k, rows, :] for k in range(mobs.shape[0])], (pulled, slot_frac, slot_drive)
    )
    new = [f + t for f, t in zip(slot_frac, sums)]
    diffus = jnp.ones(new[0].shape, jnp.float32)
    for value, d in zip(new, slot_diff):
        diffus = diffus + value * value * d
    return new, diffus


def laplacian_at(dense, phases, nz, at, pitch):
    for phase in range(phases):
        centre = dense[phase, at(0), :]
        along_x = dense[phase, at(pitch), :] + dense[phase, at(-pitch), :]
        along_y = dense[phase, at(1), :] + dense[phase, at(-1), :]
        along_z = pltpu.roll(centre, nz - 1, 1) + pltpu.roll(centre, 1, 1)
        yield (along_x + along_y + along_z) - 6.0 * centre


def interior_kernel(
    phases, shape, planes, dense, mobs, frac, ids, conc, drive, diffusivity, *refs
):
    nx, ny, nz = shape
    new_out, diff_out = refs[-2:]
    pitch = ny + 2 * SUB
    tables = tables_of(phases, drive, diffusivity, nz)

    def update(x, carry):
        for part in range(ny // SUB):
            rows = pl.ds(pl.multiple_of(x * ny, SUB) + part * SUB, SUB)
            base = pl.multiple_of((x + 1) * pitch, SUB) + (part + 1) * SUB
            laplacian = laplacian_at(
                dense, phases, nz, lambda shift, base=base: pl.ds(base + shift, SUB), pitch
            )
            new, diffus = renew(laplacian, rows, mobs, frac, ids, conc, tables)
            for s, value in enumerate(new):
                new_out[s, rows, :] = value
            diff_out[rows, :] = diffus
        return carry

    lax.fori_loop(planes[0], planes[1], update, 0)


def edge_kernel(
    phases, shape, dense, mobs, frac, ids, conc, drive, diffusivity, x_a, x_b, y_a, y_b, _,
    face_a, face_b,
):
    nx, ny, nz = shape
    pitch = ny + 2 * SUB
    tables = tables_of(phases, drive, diffusivity, nz)
    place = lax.broadcasted_iota(jnp.int32, (nx, nz), 0)
    at_a = place == jnp.where(even("gx"), nx - 1, 0)
    at_b = place == jnp.where(even("gx"), 0, nx - 1)
    up = even("gy")
    for face, halo, upper in ((face_a, y_a, up), (face_b, y_b, jnp.logical_not(up))):
        y = jnp.where(upper, ny - 1, 0)
        inner = laplacian_at(
            dense,
            phases,
            nz,
            lambda shift, y=y: pl.ds(pitch + SUB + y + shift, nx, stride=pitch),
            pitch,
        )

        def whole(inner=inner, halo=halo, y=y):
            for phase, value in enumerate(inner):
                row_a = jnp.where(at_a, x_a[phase, pl.ds(y, 1), :], 0.0)
                row_b = jnp.where(at_b, x_b[phase, pl.ds(y, 1), :], 0.0)
                yield value + halo[phase] + (row_a + row_b)

        _, diffus = renew(
            whole(), pl.ds(y, nx, stride=ny), mobs, frac, ids, conc, tables
        )
        face[...] = diffus


def outer_kernel(
    phases, shape, new_in, diff_in, mobs, ids, x_a, x_b, y_a, y_b, diffusivity, new_out, diff_out
):
    nx, ny, nz = shape
    slots = new_in.shape[0]
    diff_table = lane_table(diffusivity, nz)
    del new_in, diff_in

    def add(rows, halo):
        slot_ids = [ids[s, rows, :] for s in range(slots)]
        level = pick_slots(slot_ids, (halo(p) for p in range(phases)))
        sums = exchange(level, [mobs[k, rows, :] for k in range(mobs.shape[0])])
        diffus = jnp.ones(sums[0].shape, jnp.float32)
        for s in range(slots):
            new = new_out[s, rows, :] + sums[s]
            new_out[s, rows, :] = new
            diffus = diffus + new * new * lookup(diff_table, slot_ids[s])
        diff_out[rows, :] = diffus

    right = even("gx")
    for halo, upper in ((x_a, right), (x_b, jnp.logical_not(right))):
        base = jnp.where(upper, (nx - 1) * ny, 0)
        for part in range(ny // SUB):
            add(
                pl.ds(pl.multiple_of(base + part * SUB, SUB), SUB),
                lambda p, halo=halo, part=part: halo[p, part * SUB : (part + 1) * SUB, :],
            )
    up = even("gy")
    for halo, upper in ((y_a, up), (y_b, jnp.logical_not(up))):
        rows = pl.ds(jnp.where(upper, ny - 1, 0), nx, stride=ny)
        add(rows, lambda p, halo=halo: halo[p])


def chain_ends(source, face):
    one = jnp.ones_like(source[0])

    def sweep(values, faces):
        mass, total, through = one, values[0], one
        for value, f in zip(values[1:], faces):
            share = f / (mass + f)
            total = value + share * total
            mass = 1.0 + share * mass
            through = share * through
        unit = 1.0 / mass
        return total * unit, unit, through * unit

    last, g_last, g_through = sweep(source, face)
    first, g_first, _ = sweep(source[::-1], face[::-1])
    return first, last, g_first, g_through, g_last


def join(left, right):
    first_a, last_a, gff_a, gfl_a, gll_a, d_first, d_last = left
    first_b, last_b, gff_b, gfl_b, gll_b, d_next, d_end = right
    face = 0.5 * (d_last + d_next)
    link = face / (1.0 + face * (gll_a + gff_b))
    flux = link * (first_b - last_a)
    return (
        first_a + flux * gfl_a,
        last_b - flux * gfl_b,
        gff_a - link * gfl_a * gfl_a,
        gfl_a * link * gfl_b,
        gll_b - link * gfl_b * gfl_b,
        d_first,
        d_end,
    )


def fluxes(blocks, flux_left, flux_right):
    count = len(blocks)
    views_left = []
    first, last, gff, gfl, gll, _, d_last = blocks[0]
    view = (last - flux_left * gfl, gll, d_last)
    for m in range(count - 1):
        views_left.append(view)
        if m + 1 < count - 1:
            first, last, gff, gfl, gll, d_first, d_last = blocks[m + 1]
            face = 0.5 * (view[2] + d_first)
            link = face / (1.0 + face * (view[1] + gff))
            flux = link * (first - view[0])
            view = (last - flux * gfl, gll - link * gfl * gfl, d_last)
    views_right = []
    first, last, gff, gfl, gll, d_first, _ = blocks[-1]
    view = (first + flux_right * gfl, gff, d_first)
    for m in range(count - 1, 0, -1):
        views_right.append(view)
        if m - 1 > 0:
            first, last, gff, gfl, gll, d_first, d_last = blocks[m - 1]
            face = 0.5 * (d_last + view[2])
            link = face / (1.0 + face * (gll + view[1]))
            flux = link * (view[0] - last)
            view = (first + flux * gfl, gff - link * gfl * gfl, d_first)
    views_right = views_right[::-1]
    inner = []
    for left, right in zip(views_left, views_right):
        face = 0.5 * (left[2] + right[2])
        inner.append(face * (right[0] - left[0]) / (1.0 + face * (left[1] + right[1])))
    return [flux_left] + inner + [flux_right]


def choose(options, number):
    out = options[0]
    for k in range(1, len(options)):
        out = jnp.where(number == k, options[k], out)
    return out


def members(axis, level, refs):
    stride, radix = level
    own = lax.rem(lax.axis_index(axis) // stride, radix)
    blocks = []
    for m in range(radix):
        number = own ^ m
        blocks.append(tuple(choose([r[q] for r in refs], number) for q in range(7)))
    return own, blocks


def view(block, lower):
    ends = ((block[1], block[4], block[6]), (block[0], block[2], block[5]))
    return tuple(choose(list(pair), jnp.where(lower, 0, 1)) for pair in zip(*ends))


def solve_levels(axis, levels, refs):
    zero = jnp.zeros(refs[0].shape[1:], jnp.float32)
    lower, upper = zero, zero
    for k in range(len(levels) - 1, -1, -1):
        level, pair = levels[k], refs[2 * k : 2 * k + 2]
        if pair[1].shape[0] == 3:
            number = lax.rem(lax.axis_index(axis) // level[0], level[1])
            own = view(tuple(pair[0][q] for q in range(7)), number == 0)
            other = tuple(pair[1][q] for q in range(3))
            face = 0.5 * (own[2] + other[2])
            flux = face * (other[0] - own[0]) / (1.0 + face * (own[1] + other[1]))
            lower, upper = choose([zero, -flux], number), choose([flux, zero], number)
        else:
            number, blocks = members(axis, level, pair)
            between = fluxes(blocks, lower, upper)
            lower, upper = choose(between[:-1], number), choose(between[1:], number)
    return lower, upper


def join_kernel(axis, level, above, *refs):
    pair, outs = refs[:2], refs[-1:] if above is None else refs[-2:]
    _, blocks = members(axis, level, pair)
    total = join(*blocks)
    for q in range(7):
        outs[0][q] = total[q]
    if above is not None:
        short = view(total, lax.rem(lax.axis_index(axis) // above, 2) == 0)
        for q in range(3):
            outs[1][q] = short[q]


def gather_levels(axis, payload, shape, after=None):
    count = lax.axis_size(axis)
    levels, refs = [], []
    stride, send = 1, payload
    while stride < count:
        pairs = [(i, i ^ stride) for i in range(count)]
        levels.append((stride, 2))
        refs += [payload, lax.ppermute(send, axis, pairs)]
        stride *= 2
        if stride < count:
            above = stride if 2 * stride == count else None
            ins = refs[-2:] + ([after] if after is not None else [])
            outs = call(
                functools.partial(join_kernel, axis, levels[-1], above),
                "join_" + axis,
                [shape] + ([(3, *shape[1:])] if above else []),
                ins,
                far=range(2, len(ins)),
            )
            payload, send, after = outs[0], outs[-1], None
    return levels, refs


def flux_x_kernel(shape, diff, conc, y_a, y_b, halo_a, halo_b, payload, source, applied):
    nx, ny, nz = shape
    up = even("gy")
    place = lax.axis_index("gy")
    count = lax.axis_size("gy")
    last = y_a.shape[0] - 1

    def side(a, b, flag):
        return jnp.where(jnp.full((nx, nz), flag.astype(jnp.int32)) == 1, a, b)

    has_low = jnp.where(place > 0, 0.5, 0.0)
    has_high = jnp.where(place < count - 1, 0.5, 0.0)
    d_low = side(halo_b[...], halo_a[...], up)
    d_high = side(halo_a[...], halo_b[...], up)
    c_low = side(y_b[last], y_a[last], up)
    c_high = side(y_a[last], y_b[last], up)
    d_prev, c_prev = diff[pl.ds(0, nx, stride=ny), :], conc[pl.ds(0, nx, stride=ny), :]
    below = has_low * (d_low + d_prev) * (c_prev - c_low)
    for y in range(ny):
        if y + 1 < ny:
            d_next, c_next = diff[pl.ds(y + 1, nx, stride=ny), :], conc[pl.ds(y + 1, nx, stride=ny), :]
            above = 0.5 * (d_prev + d_next) * (c_next - c_prev)
        else:
            d_next, c_next = d_high, c_high
            above = has_high * (d_prev + d_next) * (c_next - c_prev)
        applied[pl.ds(y, nx, stride=ny), :] = above - below
        d_prev, c_prev, below = d_next, c_next, above

    inside = lax.broadcasted_iota(jnp.int32, (ny, nz), 1) < nz - 1
    rows = [slice(x * ny, (x + 1) * ny) for x in range(nx)]
    values, d = [], []
    for x in range(nx):
        here, c = diff[rows[x], :], conc[rows[x], :]
        flux = jnp.where(
            inside, 0.5 * (here + pltpu.roll(here, nz - 1, 1)) * (pltpu.roll(c, nz - 1, 1) - c), 0.0
        )
        value = (c + applied[rows[x], :]) + (flux - pltpu.roll(flux, 1, 1))
        source[rows[x], :] = value
        values.append(value)
        d.append(here)
    face = [0.5 * (a + b) for a, b in zip(d[:-1], d[1:])]
    ends = chain_ends(values, face)
    for q in range(5):
        payload[q] = ends[q]
    payload[5] = d[0]
    payload[6] = d[-1]


def inside_chain(values, face):
    one = jnp.ones_like(face[0])
    mass, total, through = one, values[0], one
    shares, totals, throughs, inverses = [], [], [], []
    for value, f in zip(values[1:], face):
        inverse = 1.0 / (mass + f)
        share = f * inverse
        shares.append(share)
        inverses.append(inverse)
        totals.append(total)
        throughs.append(through)
        total = value + share * total
        mass = 1.0 + share * mass
        through = share * through
    unit = 1.0 / mass
    base, first, last = [total * unit], [through * unit], [unit]
    for share, inverse, total, through in zip(
        shares[::-1], inverses[::-1], totals[::-1], throughs[::-1]
    ):
        base.append(inverse * total + share * base[-1])
        first.append(inverse * through + share * first[-1])
        last.append(share * last[-1])
    return base[::-1], first[::-1], last[::-1]


def inner_x_kernel(shape, diff, source, base_out, first_out, last_out):
    nx, ny, nz = shape
    for part in range(ny // SUB):
        rows = [slice(x * ny + part * SUB, x * ny + (part + 1) * SUB) for x in range(nx)]
        d = [diff[r, :] for r in rows]
        face = [0.5 * (a + b) for a, b in zip(d[:-1], d[1:])]
        base, first, last = inside_chain([source[r, :] for r in rows], face)
        for r, u, f, l in zip(rows, base, first, last):
            base_out[r, :] = u
            first_out[r, :] = f
            last_out[r, :] = l


def flux_y_kernel(shape, levels, diff, base, first, last, applied, _, *refs):
    nx, ny, nz = shape
    payload, source, section = refs[-3:]
    lower, upper = solve_levels("gx", levels, refs[:-3])
    for x in range(nx):
        r = slice(x * ny, (x + 1) * ny)
        section[r, :] = (base[r, :] + upper * last[r, :] - lower * first[r, :]) - applied[r, :]
    values = [section[pl.ds(y, nx, stride=ny), :] for y in range(ny)]
    d = [diff[pl.ds(y, nx, stride=ny), :] for y in range(ny)]
    for y in range(ny):
        source[y] = values[y]
    face = [0.5 * (a + b) for a, b in zip(d[:-1], d[1:])]
    ends = chain_ends(values, face)
    for q in range(5):
        payload[q] = ends[q]
    payload[5] = d[0]
    payload[6] = d[-1]


def inner_y_kernel(shape, diff, source, base_out, first_out, last_out):
    nx, ny, nz = shape
    d = [diff[pl.ds(y, nx, stride=ny), :] for y in range(ny)]
    face = [0.5 * (a + b) for a, b in zip(d[:-1], d[1:])]
    base, first, last = inside_chain([source[y] for y in range(ny)], face)
    for y in range(ny):
        base_out[y] = base[y]
        first_out[y] = first[y]
        last_out[y] = last[y]


def steps_of(nz):
    count = 1
    while 2**count < nz:
        count += 1
    return count


def coefficients_z_kernel(shape, diff, conc, applied, start, left_out, right_out, unit_out):
    nx, ny, nz = shape
    lane = lax.broadcasted_iota(jnp.int32, (nx, nz), 1)

    state = []
    for y in range(ny):
        rows = pl.ds(y, nx, stride=ny)
        d, c = diff[rows, :], conc[rows, :]
        right = jnp.where(lane < nz - 1, 0.5 * (d + pltpu.roll(d, nz - 1, 1)), 0.0)
        left = pltpu.roll(right, 1, 1)
        flux = right * (pltpu.roll(c, nz - 1, 1) - c)
        applied[y] = flux - pltpu.roll(flux, 1, 1)
        mass = jnp.ones((nx, nz), jnp.float32)
        unit = 1.0 / (mass + left + right)
        start[y] = unit
        state.append((mass, left, right, unit))
    for step in range(steps_of(nz)):
        shift = 2**step
        for y in range(ny):
            mass, left, right, unit = state[y]
            mass, left, right = mass * unit, left * unit, right * unit
            mass = mass + left * pltpu.roll(mass, shift, 1) + right * pltpu.roll(mass, nz - shift, 1)
            wide_left = left * pltpu.roll(left, shift, 1)
            wide_right = right * pltpu.roll(right, nz - shift, 1)
            unit = 1.0 / (mass + wide_left + wide_right) if 2 * shift < nz else 1.0 / mass
            left_out[step, y] = left * unit
            right_out[step, y] = right * unit
            unit_out[step, y] = unit
            state[y] = mass, wide_left, wide_right, unit


def last_kernel(shape, levels, applied, start, left, right, unit, base, first, last, *refs):
    nx, ny, nz = shape
    out = refs[-1]
    lower, upper = solve_levels("gy", levels, refs[:-1])
    values = [
        ((base[y] + upper * last[y] - lower * first[y]) - applied[y]) * start[y] for y in range(ny)
    ]
    for step in range(steps_of(nz)):
        shift = 2**step
        values = [
            unit[step, y] * v
            + left[step, y] * pltpu.roll(v, shift, 1)
            + right[step, y] * pltpu.roll(v, nz - shift, 1)
            for y, v in enumerate(values)
        ]
    for y in range(ny):
        out[pl.ds(y, nx, stride=ny), :] = values[y]


def commit_kernel(new, out, sem):
    copy = pltpu.make_async_copy(new, out, sem)
    copy.start()
    copy.wait()


def exchange_near(axis, array):
    count = lax.axis_size(axis)
    return lax.ppermute(array, axis, [(i, i ^ 1) for i in range(count)])


def exchange_far(axis, array):
    count = lax.axis_size(axis)
    pairs = [(i, (i - 1) % count if i % 2 == 0 else (i + 1) % count) for i in range(count)]
    return lax.ppermute(array, axis, pairs)


def body(phase_frac, phase_ids, conc, pair_class, mobility, drive, diffusivity):
    slots, nx, ny, nz = phase_frac.shape
    phases = drive.shape[0]
    shape = (nx, ny, nz)
    cells = nx * ny
    flat = (cells, nz)
    frac = far_away(phase_frac.reshape(slots, cells, nz))
    ids = far_away(phase_ids.reshape(slots, cells, nz))
    field = far_away(conc.reshape(cells, nz))

    small = [pair_class] + [v.reshape(1, -1) for v in (mobility, drive, diffusivity)]
    ins = [frac, ids, field] + [far_away(v) for v in small]
    frac, ids, field, classes, mobility, drive, diffusivity, x_a, x_b = call(
        functools.partial(first_kernel, phases, shape),
        "first",
        [jax.ShapeDtypeStruct(v.shape, v.dtype) for v in ins] + [(phases, ny, nz)] * 2,
        ins,
        scratch=[
            pltpu.VMEM((2, slots, ny, nz), jnp.float32),
            pltpu.VMEM((2, slots, ny, nz), ids.dtype),
            pltpu.SemaphoreType.DMA((len(ins) + 6,)),
        ],
        far=range(len(ins)),
    )
    x_a = exchange_near("gx", x_a)
    x_b = exchange_far("gx", x_b)
    y_a, y_b = call(
        functools.partial(faces_kernel, phases, shape),
        "faces",
        [(phases + 1, nx, nz)] * 2,
        [frac, ids, field],
    )
    y_b = exchange_far("gy", y_b)
    y_a = exchange_near("gy", y_a)
    dense, mobs = call(
        functools.partial(build_kernel, phases, shape),
        "build",
        [(phases, (nx + 2) * (ny + 2 * SUB), nz), (len(pairs_of(slots)), cells, nz)],
        [frac, ids, classes, mobility],
    )
    fields = [dense, mobs, frac, ids, field, drive, diffusivity]
    middle = nx // 2
    new, diffus = call(
        functools.partial(interior_kernel, phases, shape, (0, middle)),
        "interior_low",
        [(slots, cells, nz), flat],
        fields,
    )
    faces = call(
        functools.partial(edge_kernel, phases, shape),
        "edge",
        [(nx, nz)] * 2,
        fields + [x_a, x_b, y_a, y_b, diffus],
    )
    face_b = exchange_far("gy", faces[1])
    face_a = exchange_near("gy", faces[0])
    new, diffus = call(
        functools.partial(interior_kernel, phases, shape, (middle, nx)),
        "interior_high",
        [(slots, cells, nz), flat],
        fields + [new, diffus, faces[0]],
        aliases={7: 0, 8: 1},
    )
    new, diffus = call(
        functools.partial(outer_kernel, phases, shape),
        "outer",
        [(slots, cells, nz), flat],
        [new, diffus, mobs, ids, x_a, x_b, y_a, y_b, diffusivity],
        aliases={0: 0, 1: 1},
    )
    payload, source, applied = call(
        functools.partial(flux_x_kernel, shape),
        "flux_x",
        [(7, ny, nz), flat, flat],
        [diffus, field, y_a, y_b, face_a, face_b],
    )
    (new,) = pl.pallas_call(
        commit_kernel,
        name="commit",
        out_shape=[jax.ShapeDtypeStruct(new.shape, new.dtype)],
        in_specs=[VMEM],
        out_specs=[HBM],
        scratch_shapes=[pltpu.SemaphoreType.DMA],
        compiler_params=pltpu.CompilerParams(vmem_limit_bytes=12 << 20),
        cost_estimate=pl.CostEstimate(flops=20000000, bytes_accessed=1 << 20, transcendentals=0),
    )(new)
    levels, refs = gather_levels("gx", payload, (7, ny, nz), far_away(new))
    applied_z, start, left, right, unit = call(
        functools.partial(coefficients_z_kernel, shape),
        "coefficients_z",
        [(ny, nx, nz)] * 2 + [(steps_of(nz), ny, nx, nz)] * 3,
        [diffus, field],
    )
    base, first, last = call(
        functools.partial(inner_x_kernel, shape), "inner_x", [flat] * 3, [diffus, source]
    )
    payload, source = call(
        functools.partial(flux_y_kernel, shape, levels),
        "flux_y",
        [(7, nx, nz), (ny, nx, nz)],
        [diffus, base, first, last, applied, applied_z] + refs,
        scratch=[flat],
    )
    levels, refs = gather_levels("gy", payload, (7, nx, nz))
    base, first, last = call(
        functools.partial(inner_y_kernel, shape), "inner_y", [(ny, nx, nz)] * 3, [diffus, source]
    )
    (out,) = call(
        functools.partial(last_kernel, shape, levels),
        "last",
        [flat],
        [applied_z, start, left, right, unit, base, first, last] + refs,
    )
    return new.reshape(slots, nx, ny, nz), out.reshape(nx, ny, nz)


def solution(mesh):
    split = P(None, "gx", "gy", None)
    return jax.shard_map(
        body,
        mesh=mesh,
        in_specs=(split, split, P("gx", "gy", None), P(), P(), P(), P()),
        out_specs=(split, P("gx", "gy", None)),
        check_vma=False,
    )
```

```python
import functools

import jax
import jax.numpy as jnp
from jax import lax
from jax.experimental import pallas as pl
from jax.experimental.pallas import tpu as pltpu
from jax.sharding import PartitionSpec as P


KAPPA = 2.0
DRIVE = 4.0
SUB = 8
UNROLL = 8

VMEM = pl.BlockSpec(memory_space=pltpu.VMEM)
SMEM = pl.BlockSpec(memory_space=pltpu.SMEM)
HBM = pl.BlockSpec(memory_space=pltpu.HBM)


def call(kernel, outs, ins, scratch=(), aliases={}, cost=20000, scalars=(), far=(), out_far=False):
    f32 = jnp.float32
    place = [SMEM if i in scalars else HBM if i in far else VMEM for i in range(len(ins))]
    return pl.pallas_call(
        kernel,
        out_shape=[s if isinstance(s, jax.ShapeDtypeStruct) else jax.ShapeDtypeStruct(s, f32) for s in outs],
        in_specs=place,
        out_specs=[HBM if out_far else VMEM] * len(outs),
        scratch_shapes=[pltpu.VMEM(s, f32) if isinstance(s, tuple) else s for s in scratch],
        input_output_aliases=aliases,
        compiler_params=pltpu.CompilerParams(vmem_limit_bytes=12 << 20),
        cost_estimate=pl.CostEstimate(flops=cost * 1000, bytes_accessed=1 << 20, transcendentals=0),
    )(*ins)


def far_away(array):
    return pltpu.with_memory_space_constraint(array, pltpu.HBM)


def lookup(table, index):
    dims = lax.GatherDimensionNumbers(
        offset_dims=(),
        collapsed_slice_dims=(1,),
        start_index_map=(1,),
        operand_batching_dims=(0,),
        start_indices_batching_dims=(0,),
    )
    return lax.gather(
        table, index[..., None], dims, (1, 1), mode=lax.GatherScatterMode.PROMISE_IN_BOUNDS
    )


def lane_table(ref, nz):
    row = jnp.concatenate([ref[...]] * (nz // ref.shape[1]), axis=1)
    return jnp.broadcast_to(row, (SUB, nz))


def even(axis):
    return lax.rem(lax.axis_index(axis), 2) == 0


def pick_rows(ids, fields, count):
    rows = []
    for phase in range(count):
        total = jnp.zeros(fields[0].shape, jnp.float32)
        for slot_id, field in zip(ids, fields):
            total = jnp.where(slot_id == phase, field, total)
        rows.append(total)
    return rows


def pick_slots(ids, rows):
    rows = list(rows)
    bits = range((len(rows) - 1).bit_length())
    picked = []
    for slot_id in ids:
        level = rows
        for bit in bits:
            odd = (slot_id & (1 << bit)) != 0
            level = [
                jnp.where(odd, level[k + 1], level[k]) if k + 1 < len(level) else level[k]
                for k in range(0, len(level), 2)
            ]
        picked.append(level[0])
    return picked


def pair_base(phase, phases):
    return phase * (2 * phases - 3 - phase) // 2 - 1


def pair_table(pair_class, mobility, phases, nz):
    wide = jnp.concatenate([pair_class[...]] * (nz // phases), axis=1)
    options = lane_table(mobility, nz)
    values = jnp.concatenate(
        [lookup(options, wide[k : k + SUB]) for k in range(0, phases, SUB)], axis=0
    )
    lane = lax.broadcasted_iota(jnp.int32, (SUB, nz), 1)
    table = jnp.zeros((SUB, nz), jnp.float32)
    for p in range(phases - 1):
        base = pair_base(p, phases)
        row = jnp.broadcast_to(values[p : p + 1, :], (SUB, nz))
        shift = base % phases
        if shift:
            row = pltpu.roll(row, shift, 1)
        table = jnp.where((lane > base + p) & (lane < base + phases), row, table)
    return table


def pairs_of(count):
    return [(a, b) for a in range(count) for b in range(a + 1, count)]


def mobilities(ids, table, phases):
    base = [lax.shift_right_arithmetic(i * (2 * phases - 3 - i), 1) - 1 for i in ids]
    return [
        lookup(table, jnp.minimum(base[a], base[b]) + jnp.maximum(ids[a], ids[b]))
        for a, b in pairs_of(len(ids))
    ]


def exchange(level, mobs, source=None):
    sums = [jnp.zeros(level[0].shape, jnp.float32) for _ in level]
    for (a, b), mob in zip(pairs_of(len(level)), mobs):
        term = level[a] - level[b]
        if source is not None:
            pulled, frac, drive = source
            term = term + pulled[a] * (frac[b] * (drive[a] - drive[b]))
        term = mob * term
        sums[a] = sums[a] + term
        sums[b] = sums[b] - term
    return sums


def pitch_of(shape):
    return shape[1] + 1 + shape[1] % 2


def padded(shape):
    return -(-shape[0] * pitch_of(shape) // SUB) * SUB


def bordered(shape):
    return -(-((shape[0] + 2) * pitch_of(shape) + 1) // SUB) * SUB


def first_kernel(phases, shape, frac_far, ids_far, conc_far, *refs):
    nx, ny, _ = shape
    small_far, (frac, ids, conc, *small), x_a, x_b, dense, sems = (
        refs[:4], refs[4:11], refs[11], refs[12], refs[13], refs[14]
    )
    slots = frac.shape[0]
    half = slots // 2
    planes, rest = (slice(0, ny), slice((nx - 1) * ny, None)), slice(ny, (nx - 1) * ny)
    pieces = [
        (far.at[:, rows, :], near.at[:, rows, :])
        for rows in planes
        for far, near in ((frac_far, frac), (ids_far, ids))
    ]
    pieces += [
        (far.at[part, rest, :], near.at[part, rest, :])
        for part in (slice(0, half), slice(half, None))
        for far, near in ((frac_far, frac), (ids_far, ids))
    ]
    pieces += [(conc_far, conc), *zip(small_far, small)]
    copies = [
        pltpu.make_async_copy(far, near, sems.at[k]) for k, (far, near) in enumerate(pieces)
    ]
    for copy in copies:
        copy.start()
    for phase in range(phases):
        dense[phase] = jnp.zeros(dense.shape[1:], jnp.float32)
    for copy in copies[:4]:
        copy.wait()
    right = even("gx")
    for out, upper in ((x_a, right), (x_b, jnp.logical_not(right))):
        base = jnp.where(upper, (nx - 1) * ny, 0)
        for part in range(ny // SUB):
            rows = pl.ds(pl.multiple_of(base, SUB) + part * SUB, SUB)
            held = pick_rows(
                [ids[s, rows, :] for s in range(slots)],
                [frac[s, rows, :] for s in range(slots)],
                phases,
            )
            for phase in range(phases):
                out[phase, part * SUB : (part + 1) * SUB, :] = held[phase]
    for copy in copies[4:]:
        copy.wait()


def faces_kernel(
    phases, shape, frac, ids, conc, pair_class, mobility, drive, diffusivity, y_a, y_b, frac_y, ids_y, tables
):
    nx, ny, nz = shape
    slots = frac.shape[0]
    tables[0] = lane_table(drive, nz)
    tables[1] = lane_table(diffusivity, nz)
    tables[2] = pair_table(pair_class, mobility, phases, nz)
    up = even("gy")
    for k, (out, upper) in enumerate(((y_a, up), (y_b, jnp.logical_not(up)))):
        rows = pl.ds(jnp.where(upper, ny - 1, 0), nx, stride=ny)
        slot_ids = [ids[s, rows, :] for s in range(slots)]
        slot_frac = [frac[s, rows, :] for s in range(slots)]
        for s in range(slots):
            ids_y[k, s] = slot_ids[s]
            frac_y[k, s] = slot_frac[s]
        for phase, row in enumerate(pick_rows(slot_ids, slot_frac, phases)):
            out[phase] = row
        out[phases] = conc[rows, :]


def build_kernel(phases, shape, _, tables, frac, ids, dense, mob_out):
    nx, ny, _ = shape
    slots = frac.shape[0]
    pitch = pitch_of(shape)
    table = tables[2]

    def plane(x, carry):
        for part in range(ny // SUB):
            rows = pl.ds(pl.multiple_of(x * ny, SUB) + part * SUB, SUB)
            slot_ids = [ids[s, rows, :] for s in range(slots)]
            into = pl.ds(x * pitch + part * SUB, SUB)
            for k, mob in enumerate(mobilities(slot_ids, table, phases)):
                mob_out[k, into, :] = mob
            held = pick_rows(slot_ids, [frac[s, rows, :] for s in range(slots)], phases)
            into = pl.ds((x + 1) * pitch + 1 + part * SUB, SUB)
            for phase in range(phases):
                dense[phase, into, :] = held[phase]
        return carry

    lax.fori_loop(0, nx, plane, 0, unroll=UNROLL if nx % UNROLL == 0 else 1)


def renew(laplacian, slot_ids, slot_frac, mobs, conc, tables):
    slot_drive, slot_diff = [], []
    for i in slot_ids:
        slot_drive.append(lookup(tables[0], i))
        slot_diff.append(lookup(tables[1], i))
    curvature = pick_slots(slot_ids, laplacian)
    level = [c + KAPPA * f for c, f in zip(curvature, slot_frac)]
    scaled = DRIVE * conc
    pulled = [scaled * f for f in slot_frac]
    sums = exchange(level, mobs, (pulled, slot_frac, slot_drive))
    new = [f + t for f, t in zip(slot_frac, sums)]
    diffus = jnp.ones(new[0].shape, jnp.float32)
    for value, d in zip(new, slot_diff):
        diffus = diffus + value * value * d
    return new, diffus


def laplacian_at(dense, phases, nz, at, pitch):
    for phase in range(phases):
        centre = dense[phase, at(0), :]
        along_x = dense[phase, at(pitch), :] + dense[phase, at(-pitch), :]
        along_y = dense[phase, at(1), :] + dense[phase, at(-1), :]
        along_z = pltpu.roll(centre, nz - 1, 1) + pltpu.roll(centre, 1, 1)
        yield (along_x + along_y + along_z) - 6.0 * centre


def interior_kernel(phases, shape, planes, dense, mobs, tables, frac, ids, conc, *refs):
    _, ny, nz = shape
    slots = frac.shape[0]
    new_out, diff_out = refs[-2:]
    pitch = pitch_of(shape)

    def update(x, carry):
        for part in range(ny // SUB):
            rows = pl.ds(pl.multiple_of(x * ny, SUB) + part * SUB, SUB)
            wide = pl.ds(x * pitch + part * SUB, SUB)
            base = (x + 1) * pitch + 1 + part * SUB
            laplacian = laplacian_at(
                dense, phases, nz, lambda shift, base=base: pl.ds(base + shift, SUB), pitch
            )
            new, diffus = renew(
                laplacian,
                [ids[s, rows, :] for s in range(slots)],
                [frac[s, rows, :] for s in range(slots)],
                [mobs[k, wide, :] for k in range(mobs.shape[0])],
                conc[rows, :],
                tables,
            )
            for s, value in enumerate(new):
                new_out[s, rows, :] = value
            diff_out[wide, :] = diffus
        return carry

    steps = planes[1] - planes[0]
    lax.fori_loop(planes[0], planes[1], update, 0, unroll=2 if steps % 2 == 0 else 1)


def edge_kernel(
    phases, shape, dense, mobs, tables, frac_y, ids_y, sent_a, sent_b, x_a, x_b, y_a, y_b, _,
    face_a, face_b, new_y,
):
    nx, ny, nz = shape
    slots = frac_y.shape[1]
    pitch = pitch_of(shape)
    place = lax.broadcasted_iota(jnp.int32, (nx, nz), 0)
    at_a = place == jnp.where(even("gx"), nx - 1, 0)
    at_b = place == jnp.where(even("gx"), 0, nx - 1)
    up = even("gy")
    for k, (face, halo, sent, upper) in enumerate(
        ((face_a, y_a, sent_a, up), (face_b, y_b, sent_b, jnp.logical_not(up)))
    ):
        y = jnp.where(upper, ny - 1, 0)
        inner = laplacian_at(
            dense,
            phases,
            nz,
            lambda shift, y=y: pl.ds(pitch + 1 + y + shift, nx, stride=pitch),
            pitch,
        )

        def whole(inner=inner, halo=halo, y=y):
            for phase, value in enumerate(inner):
                row_a = jnp.where(at_a, x_a[phase, pl.ds(y, 1), :], 0.0)
                row_b = jnp.where(at_b, x_b[phase, pl.ds(y, 1), :], 0.0)
                yield value + halo[phase] + (row_a + row_b)

        new, diffus = renew(
            whole(),
            [ids_y[k, s] for s in range(slots)],
            [frac_y[k, s] for s in range(slots)],
            [mobs[m, pl.ds(y, nx, stride=pitch), :] for m in range(mobs.shape[0])],
            sent[phases],
            tables,
        )
        face[...] = diffus
        for s in range(slots):
            new_y[k, s] = new[s]


def outer_kernel(
    phases, shape, new_in, diff_in, mobs, tables, ids, x_a, x_b, face_a, face_b, new_y, new_out, diff_out
):
    del new_in, diff_in
    nx, ny, _ = shape
    slots = ids.shape[0]
    pitch = pitch_of(shape)
    right = even("gx")
    for halo, upper in ((x_a, right), (x_b, jnp.logical_not(right))):
        plane = jnp.where(upper, nx - 1, 0)
        for part in range(ny // SUB):
            rows = pl.ds(pl.multiple_of(plane * ny, SUB) + part * SUB, SUB)
            wide = pl.ds(plane * pitch + part * SUB, SUB)
            slot_ids = [ids[s, rows, :] for s in range(slots)]
            level = pick_slots(
                slot_ids, [halo[p, part * SUB : (part + 1) * SUB, :] for p in range(phases)]
            )
            sums = exchange(level, [mobs[k, wide, :] for k in range(mobs.shape[0])])
            diffus = jnp.ones(sums[0].shape, jnp.float32)
            for s in range(slots):
                new = new_out[s, rows, :] + sums[s]
                new_out[s, rows, :] = new
                diffus = diffus + new * new * lookup(tables[1], slot_ids[s])
            diff_out[wide, :] = diffus
    up = even("gy")
    for k, (face, upper) in enumerate(((face_a, up), (face_b, jnp.logical_not(up)))):
        y = jnp.where(upper, ny - 1, 0)
        for s in range(slots):
            new_out[s, pl.ds(y, nx, stride=ny), :] = new_y[k, s]
        diff_out[pl.ds(y, nx, stride=pitch), :] = face[...]


def chain_ends(source, face):
    one = jnp.ones_like(source[0])

    def sweep(values, faces):
        mass, total, through = one, values[0], one
        for value, f in zip(values[1:], faces):
            share = f / (mass + f)
            total = value + share * total
            mass = 1.0 + share * mass
            through = share * through
        unit = 1.0 / mass
        return total * unit, unit, through * unit

    last, g_last, g_through = sweep(source, face)
    first, g_first, _ = sweep(source[::-1], face[::-1])
    return first, last, g_first, g_through, g_last


def join(left, right):
    first_a, last_a, gff_a, gfl_a, gll_a, d_first, d_last = left
    first_b, last_b, gff_b, gfl_b, gll_b, d_next, d_end = right
    face = 0.5 * (d_last + d_next)
    link = face / (1.0 + face * (gll_a + gff_b))
    flux = link * (first_b - last_a)
    return (
        first_a + flux * gfl_a,
        last_b - flux * gfl_b,
        gff_a - link * gfl_a * gfl_a,
        gfl_a * link * gfl_b,
        gll_b - link * gfl_b * gfl_b,
        d_first,
        d_end,
    )


def fluxes(blocks, flux_left, flux_right):
    count = len(blocks)
    views_left = []
    first, last, gff, gfl, gll, _, d_last = blocks[0]
    view = (last - flux_left * gfl, gll, d_last)
    for m in range(count - 1):
        views_left.append(view)
        if m + 1 < count - 1:
            first, last, gff, gfl, gll, d_first, d_last = blocks[m + 1]
            face = 0.5 * (view[2] + d_first)
            link = face / (1.0 + face * (view[1] + gff))
            flux = link * (first - view[0])
            view = (last - flux * gfl, gll - link * gfl * gfl, d_last)
    views_right = []
    first, last, gff, gfl, gll, d_first, _ = blocks[-1]
    view = (first + flux_right * gfl, gff, d_first)
    for m in range(count - 1, 0, -1):
        views_right.append(view)
        if m - 1 > 0:
            first, last, gff, gfl, gll, d_first, d_last = blocks[m - 1]
            face = 0.5 * (d_last + view[2])
            link = face / (1.0 + face * (gll + view[1]))
            flux = link * (view[0] - last)
            view = (first + flux * gfl, gff - link * gfl * gfl, d_first)
    views_right = views_right[::-1]
    inner = []
    for left, right in zip(views_left, views_right):
        face = 0.5 * (left[2] + right[2])
        inner.append(face * (right[0] - left[0]) / (1.0 + face * (left[1] + right[1])))
    return [flux_left] + inner + [flux_right]


def choose(options, number):
    out = options[0]
    for k in range(1, len(options)):
        out = jnp.where(number == k, options[k], out)
    return out


def members(axis, level, refs):
    stride, radix = level
    own = lax.rem(lax.axis_index(axis) // stride, radix)
    blocks = []
    for m in range(radix):
        number = own ^ m
        blocks.append(tuple(choose([r[q] for r in refs], number) for q in range(7)))
    return own, blocks


def view(block, lower):
    ends = ((block[1], block[4], block[6]), (block[0], block[2], block[5]))
    return tuple(choose(list(pair), jnp.where(lower, 0, 1)) for pair in zip(*ends))


def solve_levels(axis, levels, refs):
    zero = jnp.zeros(refs[0].shape[1:], jnp.float32)
    lower, upper = zero, zero
    for k in range(len(levels) - 1, -1, -1):
        level, pair = levels[k], refs[2 * k : 2 * k + 2]
        if pair[1].shape[0] == 3:
            number = lax.rem(lax.axis_index(axis) // level[0], level[1])
            own = view(tuple(pair[0][q] for q in range(7)), number == 0)
            other = tuple(pair[1][q] for q in range(3))
            face = 0.5 * (own[2] + other[2])
            flux = face * (other[0] - own[0]) / (1.0 + face * (own[1] + other[1]))
            lower, upper = choose([zero, -flux], number), choose([flux, zero], number)
        else:
            number, blocks = members(axis, level, pair)
            between = fluxes(blocks, lower, upper)
            lower, upper = choose(between[:-1], number), choose(between[1:], number)
    return lower, upper


def join_kernel(axis, level, above, *refs):
    pair, outs = refs[:2], refs[-1:] if above is None else refs[-2:]
    _, blocks = members(axis, level, pair)
    total = join(*blocks)
    for q in range(7):
        outs[0][q] = total[q]
    if above is not None:
        short = view(total, lax.rem(lax.axis_index(axis) // above, 2) == 0)
        for q in range(3):
            outs[1][q] = short[q]


def gather_levels(axis, payload, shape, after=None):
    count = lax.axis_size(axis)
    levels, refs = [], []
    stride, send = 1, payload
    while stride < count:
        pairs = [(i, i ^ stride) for i in range(count)]
        levels.append((stride, 2))
        refs += [payload, lax.ppermute(send, axis, pairs)]
        stride *= 2
        if stride < count:
            above = stride if 2 * stride == count else None
            ins = refs[-2:] + ([after] if after is not None else [])
            outs = call(
                functools.partial(join_kernel, axis, levels[-1], above),
                [shape] + ([(3, *shape[1:])] if above else []),
                ins,
                far=range(2, len(ins)),
            )
            payload, send, after = outs[0], outs[-1], None
    return levels, refs


def flux_x_kernel(shape, diff, conc, y_a, y_b, halo_a, halo_b, payload, source, applied):
    nx, ny, nz = shape
    up = even("gy")
    place = lax.axis_index("gy")
    count = lax.axis_size("gy")
    last = y_a.shape[0] - 1

    def side(a, b, flag):
        return jnp.where(jnp.full((nx, nz), flag.astype(jnp.int32)) == 1, a, b)

    has_low = jnp.where(place > 0, 0.5, 0.0)
    has_high = jnp.where(place < count - 1, 0.5, 0.0)
    d_low = side(halo_b[...], halo_a[...], up)
    d_high = side(halo_a[...], halo_b[...], up)
    c_low = side(y_b[last], y_a[last], up)
    c_high = side(y_a[last], y_b[last], up)
    pitch = pitch_of(shape)
    d_prev, c_prev = diff[pl.ds(0, nx, stride=pitch), :], conc[pl.ds(0, nx, stride=ny), :]
    below = has_low * (d_low + d_prev) * (c_prev - c_low)
    for y in range(ny):
        if y + 1 < ny:
            d_next, c_next = diff[pl.ds(y + 1, nx, stride=pitch), :], conc[pl.ds(y + 1, nx, stride=ny), :]
            above = 0.5 * (d_prev + d_next) * (c_next - c_prev)
        else:
            d_next, c_next = d_high, c_high
            above = has_high * (d_prev + d_next) * (c_next - c_prev)
        applied[pl.ds(y, nx, stride=pitch), :] = above - below
        d_prev, c_prev, below = d_next, c_next, above

    inside = lax.broadcasted_iota(jnp.int32, (ny, nz), 1) < nz - 1
    rows = [slice(x * ny, (x + 1) * ny) for x in range(nx)]
    values, d = [], []
    for x in range(nx):
        wide = slice(x * pitch, x * pitch + ny)
        here, c = diff[wide, :], conc[rows[x], :]
        flux = jnp.where(
            inside, 0.5 * (here + pltpu.roll(here, nz - 1, 1)) * (pltpu.roll(c, nz - 1, 1) - c), 0.0
        )
        value = (c + applied[wide, :]) + (flux - pltpu.roll(flux, 1, 1))
        source[rows[x], :] = value
        values.append(value)
        d.append(here)
    face = [0.5 * (a + b) for a, b in zip(d[:-1], d[1:])]
    ends = chain_ends(values, face)
    for q in range(5):
        payload[q] = ends[q]
    payload[5] = d[0]
    payload[6] = d[-1]


def inside_chain(values, face):
    one = jnp.ones_like(face[0])
    mass, total, through = one, values[0], one
    shares, totals, throughs, inverses = [], [], [], []
    for value, f in zip(values[1:], face):
        inverse = 1.0 / (mass + f)
        share = f * inverse
        shares.append(share)
        inverses.append(inverse)
        totals.append(total)
        throughs.append(through)
        total = value + share * total
        mass = 1.0 + share * mass
        through = share * through
    unit = 1.0 / mass
    base, first, last = [total * unit], [through * unit], [unit]
    for share, inverse, total, through in zip(
        shares[::-1], inverses[::-1], totals[::-1], throughs[::-1]
    ):
        base.append(inverse * total + share * base[-1])
        first.append(inverse * through + share * first[-1])
        last.append(share * last[-1])
    return base[::-1], first[::-1], last[::-1]


def inner_x_kernel(shape, diff, source, base_out, first_out, last_out):
    nx, ny, _ = shape
    pitch = pitch_of(shape)
    for part in range(ny // SUB):
        rows = [slice(x * ny + part * SUB, x * ny + (part + 1) * SUB) for x in range(nx)]
        d = [diff[x * pitch + part * SUB : x * pitch + (part + 1) * SUB, :] for x in range(nx)]
        face = [0.5 * (a + b) for a, b in zip(d[:-1], d[1:])]
        base, first, last = inside_chain([source[r, :] for r in rows], face)
        for r, u, f, l in zip(rows, base, first, last):
            base_out[r, :] = u
            first_out[r, :] = f
            last_out[r, :] = l


def flux_y_kernel(shape, levels, diff, base, first, last, applied, _, *refs):
    nx, ny, _ = shape
    pitch = pitch_of(shape)
    payload, source, section = refs[-3:]
    lower, upper = solve_levels("gx", levels, refs[:-3])
    for x in range(nx):
        r, wide = slice(x * ny, (x + 1) * ny), slice(x * pitch, x * pitch + ny)
        section[wide, :] = (base[r, :] + upper * last[r, :] - lower * first[r, :]) - applied[wide, :]
    values = [section[pl.ds(y, nx, stride=pitch), :] for y in range(ny)]
    d = [diff[pl.ds(y, nx, stride=pitch), :] for y in range(ny)]
    for y in range(ny):
        source[y] = values[y]
    face = [0.5 * (a + b) for a, b in zip(d[:-1], d[1:])]
    ends = chain_ends(values, face)
    for q in range(5):
        payload[q] = ends[q]
    payload[5] = d[0]
    payload[6] = d[-1]


def inner_y_kernel(shape, diff, source, base_out, first_out, last_out):
    nx, ny, _ = shape
    d = [diff[pl.ds(y, nx, stride=pitch_of(shape)), :] for y in range(ny)]
    face = [0.5 * (a + b) for a, b in zip(d[:-1], d[1:])]
    base, first, last = inside_chain([source[y] for y in range(ny)], face)
    for y in range(ny):
        base_out[y] = base[y]
        first_out[y] = first[y]
        last_out[y] = last[y]


def steps_of(nz):
    count = 1
    while 2**count < nz:
        count += 1
    return count


def coefficients_z_kernel(shape, diff, conc, applied, start, left_out, right_out, unit_out):
    nx, ny, nz = shape
    lane = lax.broadcasted_iota(jnp.int32, (nx, nz), 1)

    state = []
    for y in range(ny):
        d, c = diff[pl.ds(y, nx, stride=pitch_of(shape)), :], conc[pl.ds(y, nx, stride=ny), :]
        right = jnp.where(lane < nz - 1, 0.5 * (d + pltpu.roll(d, nz - 1, 1)), 0.0)
        left = pltpu.roll(right, 1, 1)
        flux = right * (pltpu.roll(c, nz - 1, 1) - c)
        applied[y] = flux - pltpu.roll(flux, 1, 1)
        mass = jnp.ones((nx, nz), jnp.float32)
        unit = 1.0 / (mass + left + right)
        start[y] = unit
        state.append((mass, left, right, unit))
    for step in range(steps_of(nz)):
        shift = 2**step
        for y in range(ny):
            mass, left, right, unit = state[y]
            mass, left, right = mass * unit, left * unit, right * unit
            mass = mass + left * pltpu.roll(mass, shift, 1) + right * pltpu.roll(mass, nz - shift, 1)
            wide_left = left * pltpu.roll(left, shift, 1)
            wide_right = right * pltpu.roll(right, nz - shift, 1)
            unit = 1.0 / (mass + wide_left + wide_right) if 2 * shift < nz else 1.0 / mass
            left_out[step, y] = left * unit
            right_out[step, y] = right * unit
            unit_out[step, y] = unit
            state[y] = mass, wide_left, wide_right, unit


def last_kernel(shape, levels, applied, start, left, right, unit, base, first, last, *refs):
    _, ny, nz = shape
    out, held, sems = refs[-3:]
    lower, upper = solve_levels("gy", levels, refs[:-3])
    groups = [range(at, min(at + SUB, ny)) for at in range(0, ny, SUB)]
    copies = []
    for g, group in enumerate(groups):
        values = [
            ((base[y] + upper * last[y] - lower * first[y]) - applied[y]) * start[y] for y in group
        ]
        for step in range(steps_of(nz)):
            shift = 2**step
            values = [
                unit[step, y] * v
                + left[step, y] * pltpu.roll(v, shift, 1)
                + right[step, y] * pltpu.roll(v, nz - shift, 1)
                for y, v in zip(group, values)
            ]
        for y, value in zip(group, values):
            held[:, y, :] = value
        part = slice(group[0], group[-1] + 1)
        copies.append(pltpu.make_async_copy(held.at[:, part, :], out.at[:, part, :], sems.at[g]))
        copies[-1].start()
    for copy in copies:
        copy.wait()


def commit_kernel(new, out, sem):
    copy = pltpu.make_async_copy(new, out, sem)
    copy.start()
    copy.wait()


def exchange_near(axis, array):
    count = lax.axis_size(axis)
    return lax.ppermute(array, axis, [(i, i ^ 1) for i in range(count)])


def exchange_far(axis, array):
    count = lax.axis_size(axis)
    pairs = [(i, (i - 1) % count if i % 2 == 0 else (i + 1) % count) for i in range(count)]
    return lax.ppermute(array, axis, pairs)


def body(phase_frac, phase_ids, conc, pair_class, mobility, drive, diffusivity):
    slots, nx, ny, nz = phase_frac.shape
    phases = drive.shape[0]
    shape = (nx, ny, nz)
    cells = nx * ny
    flat = (cells, nz)
    frac = far_away(phase_frac.reshape(slots, cells, nz))
    ids = far_away(phase_ids.reshape(slots, cells, nz))
    field = far_away(conc.reshape(cells, nz))

    small = [pair_class] + [v.reshape(1, -1) for v in (mobility, drive, diffusivity)]
    ins = [frac, ids, field] + [far_away(v) for v in small]
    wide, block = (padded(shape), nz), (phases, bordered(shape), nz)
    frac, ids, field, *small, x_a, x_b, dense = call(
        functools.partial(first_kernel, phases, shape),
        [jax.ShapeDtypeStruct(v.shape, v.dtype) for v in ins]
        + [(phases, ny, nz)] * 2
        + [block],
        ins,
        scratch=[pltpu.SemaphoreType.DMA((13,))],
        far=range(len(ins)),
    )
    x_a = exchange_near("gx", x_a)
    x_b = exchange_far("gx", x_b)
    sent_a, sent_b, frac_y, ids_y, tables = call(
        functools.partial(faces_kernel, phases, shape),
        [(phases + 1, nx, nz)] * 2
        + [(2, slots, nx, nz), jax.ShapeDtypeStruct((2, slots, nx, nz), ids.dtype)]
        + [(3, SUB, nz)],
        [frac, ids, field, *small],
    )
    y_b = exchange_far("gy", sent_b)
    y_a = exchange_near("gy", sent_a)
    dense, mobs = call(
        functools.partial(build_kernel, phases, shape),
        [block, (len(pairs_of(slots)), *wide)],
        [dense, tables, frac, ids],
        aliases={0: 0},
    )
    fields = [dense, mobs, tables, frac, ids, field]
    middle = nx // 2
    new, diffus = call(
        functools.partial(interior_kernel, phases, shape, (0, middle)),
        [(slots, cells, nz), wide],
        fields,
    )
    *faces, new_y = call(
        functools.partial(edge_kernel, phases, shape),
        [(nx, nz)] * 2 + [(2, slots, nx, nz)],
        [dense, mobs, tables, frac_y, ids_y, sent_a, sent_b, x_a, x_b, y_a, y_b, diffus],
    )
    face_b = exchange_far("gy", faces[1])
    face_a = exchange_near("gy", faces[0])
    new, diffus = call(
        functools.partial(interior_kernel, phases, shape, (middle, nx)),
        [(slots, cells, nz), wide],
        fields + [new, diffus, faces[0]],
        aliases={6: 0, 7: 1},
    )
    new, diffus = call(
        functools.partial(outer_kernel, phases, shape),
        [(slots, cells, nz), wide],
        [new, diffus, mobs, tables, ids, x_a, x_b, *faces, new_y],
        aliases={0: 0, 1: 1},
    )
    payload, source, applied = call(
        functools.partial(flux_x_kernel, shape),
        [(7, ny, nz), flat, wide],
        [diffus, field, y_a, y_b, face_a, face_b],
    )
    (new,) = pl.pallas_call(
        commit_kernel,
        name="commit",
        out_shape=[jax.ShapeDtypeStruct(new.shape, new.dtype)],
        in_specs=[VMEM],
        out_specs=[HBM],
        scratch_shapes=[pltpu.SemaphoreType.DMA],
        compiler_params=pltpu.CompilerParams(vmem_limit_bytes=12 << 20),
        cost_estimate=pl.CostEstimate(flops=20000000, bytes_accessed=1 << 20, transcendentals=0),
    )(new)
    levels, refs = gather_levels("gx", payload, (7, ny, nz), far_away(new))
    applied_z, start, left, right, unit = call(
        functools.partial(coefficients_z_kernel, shape),
        [(ny, nx, nz)] * 2 + [(steps_of(nz), ny, nx, nz)] * 3,
        [diffus, field],
    )
    base, first, last = call(functools.partial(inner_x_kernel, shape), [flat] * 3, [diffus, source])
    payload, source = call(
        functools.partial(flux_y_kernel, shape, levels),
        [(7, nx, nz), (ny, nx, nz)],
        [diffus, base, first, last, applied, applied_z] + refs,
        scratch=[wide],
    )
    levels, refs = gather_levels("gy", payload, (7, nx, nz))
    base, first, last = call(
        functools.partial(inner_y_kernel, shape), [(ny, nx, nz)] * 3, [diffus, source]
    )
    (out,) = call(
        functools.partial(last_kernel, shape, levels),
        [(nx, ny, nz)],
        [applied_z, start, left, right, unit, base, first, last] + refs,
        scratch=[(nx, ny, nz), pltpu.SemaphoreType.DMA((-(-ny // SUB),))],
        out_far=True,
    )
    return new.reshape(slots, nx, ny, nz), out


def solution(mesh):
    split = P(None, "gx", "gy", None)

    return jax.shard_map(
        body,
        mesh=mesh,
        in_specs=(split, split, P("gx", "gy", None), P(), P(), P(), P()),
        out_specs=(split, P("gx", "gy", None)),
        check_vma=False,
    )
```
